512 devices in a mesh: dp: 16 (over z), gy: 4 (over y_lo, core), gz: 8 (over x, y_hi).
Axes of the slice: x: 4, y: 4 (y_hi: 2, y_lo: 2; y = y_hi * 2 + y_lo), z: 16, core: 2. Of those that a mesh axis runs over, the one named last changes fastest.
Arguments:
- volume: bfloat16 [16, 4, 16, 128, 128], P('dp', None, 'gy', 'gz'), may hold values from -6 to 6
- pooled_first: bfloat16 [16, 16, 8, 64, 64], P('dp', None, 'gy', 'gz'), may hold values from -6 to 6
- where_first: int32 [16, 16, 8, 64, 64], P('dp', None, 'gy', 'gz'), may hold values from 0 to 7
- pooled_second: bfloat16 [16, 32, 4, 32, 32], P('dp', None, 'gy', 'gz'), may hold values from -6 to 6
- where_second: int32 [16, 32, 4, 32, 32], P('dp', None, 'gy', 'gz'), may hold values from 0 to 7
- upstream: bfloat16 [16, 32, 4, 32, 32], P('dp', None, 'gy', 'gz'), may hold values from -6 to 6
- kernel_first: bfloat16 [16, 4, 3, 3, 3], replicated, may hold values from -0.625 to 0.625
- kernel_second: bfloat16 [32, 16, 3, 3, 3], replicated, may hold values from -0.3125 to 0.3125
Outputs:
- grad_volume: bfloat16 [16, 4, 16, 128, 128], P('dp', None, 'gy', 'gz')
- grad_kernel_first: float32 [1728], P('dp')
- grad_kernel_second: float32 [13824], P('dp')
The draws below stay inside these ranges and needn't reach their ends.
All inputs are finite; a program needn't handle non-finite values.
Results may differ from the reference program's by a relative error of at most 0.005.
Values may be sent and summed in bfloat16 or wider, within the bound.
A program may use at most 64 MiB of HBM per device.

```python
import math
import jax
import jax.numpy as jnp
from jax import lax

C0 = 4
C1 = 16
C2 = 32
NX = 128
VOLUMES = 16
NY = 16
NZ = 128


def touch_ends(result, key, smallest, largest):
    shape = result.shape
    index_at = [jax.random.randint(jax.random.fold_in(key, axis), (), 0, shape[axis]) for axis in range(len(shape))]
    result = result.at[tuple(index_at)].set(smallest)
    longest = shape.index(max(shape))
    index_at[longest] = (index_at[longest] + 1) % shape[longest]
    return result.at[tuple(index_at)].set(largest)


def levels(rng, extent, split, low, high):
    gain, own = 1.0, jax.random.fold_in(rng, 6)
    for axis_at, blocks in split:
        steps = jnp.exp(jax.random.uniform(jax.random.fold_in(own, axis_at), (blocks,), jnp.float32, low / len(split), high / len(split)))
        gain = gain * jnp.repeat(steps, extent[axis_at] // blocks).reshape([-1 if axis == axis_at else 1 for axis in range(len(extent))])
    return gain


def gaussian(stream_key, shape, scale, bound, shards=(), dtype=jnp.bfloat16):
    gain = levels(stream_key, shape, shards, -0.22, 0.18) if shards else 1.0
    result = jax.random.normal(stream_key, shape, jnp.float32) * scale * gain
    return jnp.minimum(jnp.maximum(result, -bound), bound).astype(dtype)


def setup_inputs(seed: int = 0) -> dict:
    key_of = jax.random.split(jax.random.key(seed), 9)
    volume = gaussian(key_of[0], (VOLUMES, C0, NY, NZ, NX), 1.0, 6.0, ((0, 16), (2, 4), (3, 8)))
    pooled_first = gaussian(key_of[1], (VOLUMES, C1, NY // 2, NZ // 2, NX // 2), 1.0, 6.0, ((0, 16), (2, 4), (3, 8)))
    where_first = touch_ends(jax.random.randint(key_of[2], (VOLUMES, C1, NY // 2, NZ // 2, NX // 2), 0, 8), jax.random.fold_in(key_of[2], 1), 0, 7).astype(jnp.int32)
    pooled_second = gaussian(key_of[3], (VOLUMES, C2, NY // 4, NZ // 4, NX // 4), 1.0, 6.0, ((0, 16), (2, 4), (3, 8)))
    where_second = touch_ends(jax.random.randint(key_of[4], (VOLUMES, C2, NY // 4, NZ // 4, NX // 4), 0, 8), jax.random.fold_in(key_of[4], 1), 0, 7).astype(jnp.int32)
    upstream = gaussian(key_of[5], (VOLUMES, C2, NY // 4, NZ // 4, NX // 4), 1.0, 6.0, ((0, 16), (2, 4), (3, 8)))
    kernel_first = gaussian(key_of[6], (C1, C0, 3, 3, 3), (27 * C0) ** -0.5, 0.625)
    kernel_second = gaussian(key_of[7], (C2, C1, 3, 3, 3), (27 * C1) ** -0.5, 0.3125)
    return {"volume": volume, "pooled_first": pooled_first, "where_first": where_first, "pooled_second": pooled_second, "where_second": where_second, "upstream": upstream, "kernel_first": kernel_first, "kernel_second": kernel_second}


leak_rate = 0.3

def slope_of(pre):
    return jnp.where(pre > 0, 1.0, leak_rate).astype(jnp.float32)

def unpool(values, where):
    parts = [jnp.where(where == k, values, jnp.zeros_like(values)) for k in range(8)]
    stacked = jnp.stack(parts, axis=-1)
    b, c, y, z, x = values.shape
    stacked = stacked.reshape(b, c, y, z, x, 2, 2, 2)
    stacked = jnp.transpose(stacked, (0, 1, 2, 5, 3, 6, 4, 7))
    return stacked.reshape(b, c, 2 * y, 2 * z, 2 * x).astype(jnp.bfloat16)

def input_grad(grad, kernel):
    flipped = jnp.transpose(kernel[:, :, ::-1, ::-1, ::-1], (1, 0, 2, 3, 4)).astype(jnp.float32)
    return lax.conv_general_dilated(grad.astype(jnp.float32), flipped, (1, 1, 1), ((1, 1), (1, 1), (1, 1)), dimension_numbers=('NCDHW', 'OIDHW', 'NCDHW'), precision=lax.Precision.HIGHEST)

def weight_grad(grad, source):
    b, o, y, z, x = grad.shape
    padded = jnp.pad(source.astype(jnp.float32), ((0, 0), (0, 0), (1, 1), (1, 1), (1, 1)))
    upper = grad.astype(jnp.float32)
    taps = []
    for ty in range(3):
        for tz in range(3):
            for tx in range(3):
                shifted = padded[:, :, ty:ty + y, tz:tz + z, tx:tx + x]
                taps.append(jnp.einsum('boyzx,biyzx->oi', upper, shifted, precision=lax.Precision.HIGHEST))
    return jnp.stack(taps, axis=-1).reshape(-1)

def reference(volume, pooled_first, where_first, pooled_second, where_second, upstream, kernel_first, kernel_second):

    def one_volume(items):
        vol, first, wfirst, second, wsecond, grad_out = items
        vol, first, wfirst = (vol[None], first[None], wfirst[None])
        second, wsecond, grad_out = (second[None], wsecond[None], grad_out[None])
        grad_pre2 = unpool(grad_out.astype(jnp.float32) * slope_of(second), wsecond)
        first_f = first.astype(jnp.float32)
        input_second = jnp.where(first_f > 0, first_f, leak_rate * first_f).astype(jnp.bfloat16)
        second_grad = weight_grad(grad_pre2, input_second)
        grad_pooled = input_grad(grad_pre2, kernel_second)
        grad_pre1 = unpool(grad_pooled * slope_of(first), wfirst)
        first_grad = weight_grad(grad_pre1, vol)
        grad_vol = input_grad(grad_pre1, kernel_first).astype(jnp.bfloat16)
        return (grad_vol[0], first_grad, second_grad)
    grad_vol, first_all, second_all = lax.map(one_volume, (volume, pooled_first, where_first, pooled_second, where_second, upstream))
    total = VOLUMES * NY * NZ * NX
    first_out = lax.optimization_barrier(jnp.sum(first_all, axis=0)) * math.sqrt(8.0 / total)
    second_out = lax.optimization_barrier(jnp.sum(second_all, axis=0)) * math.sqrt(64.0 / total)
    return (grad_vol, first_out, second_out)
```

```python
import functools
import math

import jax
import jax.numpy as jnp
from jax import lax
from jax.experimental import pallas as pl
from jax.experimental.pallas import tpu as pltpu
from jax.sharding import PartitionSpec as P

MESH = pl.DeviceIdType.MESH
f32, bf16, i32 = jnp.float32, jnp.bfloat16, jnp.int32
LEAK = 0.3
L = 128
NA, NB, NC = 32, 16, 4
HY, HZ = 2, 8
FY, FZ = 4, 16


def iota(shape, dim):
    return lax.broadcasted_iota(i32, shape, dim)


def dot(a, b):
    return lax.dot_general(a, b, (((1,), (0,)), ((), ())), preferred_element_type=f32)


def dot_t(a, b, precision=None):
    return lax.dot_general(
        a, b, (((1,), (1,)), ((), ())), preferred_element_type=f32, precision=precision
    )


def one_hot(mask):
    return jnp.where(mask, 1.0, 0.0).astype(bf16)


def slope_of(pre):
    return jnp.where(pre > 0, 1.0, LEAK).astype(f32)


def moved(value, by):
    lane = iota(value.shape, 1)
    inside = lane >= by if by > 0 else lane < L + by
    return jnp.where(inside, pltpu.roll(value, by % L, 1), 0.0)


def spread_across_x(value, by):
    return [moved(value[:, at : at + L], by) for at in range(0, value.shape[1], L)]


def kernel(
    sizes,
    scales,
    vol,
    first,
    where_first,
    second,
    where_second,
    upstream,
    k1,
    k2,
    grad_vol,
    out,
    g2,
    g1,
    w2,
    w1,
    a3,
    v3,
    s2,
    s1,
    msg,
    rz,
    ry,
    rg,
    sems,
    sem_z,
    sem_y,
    sem_g,
):
    ndp, ngy, ngz = sizes
    dp, gy, gz = lax.axis_index("dp"), lax.axis_index("gy"), lax.axis_index("gz")

    def at(index, step, count):
        return lax.rem(index + (step + count), count)

    def device(d=0, y=0, z=0):
        return {"dp": at(dp, d, ndp), "gy": at(gy, y, ngy), "gz": at(gz, z, ngz)}

    around = [(y, z) for y in (-1, 0, 1) for z in (-1, 0, 1) if (y, z) != (0, 0)]
    partners = [device(d=d) for d in range(1, ndp)]
    partners += [device(y=y, z=z) for y, z in around]
    partners += [device(y=y) for y in range(1, ngy)]
    partners += [device(z=z) for z in range(1, ngz)]
    barrier = pltpu.get_barrier_semaphore()
    for one in partners:
        pl.semaphore_signal(barrier, inc=1, device_id=one, device_id_type=MESH)

    upf = upstream[...].astype(f32)
    e2 = (upf * slope_of(second[...].astype(f32))).astype(bf16).astype(f32)
    p2 = where_second[...].astype(f32)
    quarter = jnp.concatenate(
        [e2[:, z] for z in range(HZ // 2)] + [p2[:, z] for z in range(HZ // 2)], axis=0
    ).astype(bf16)
    by4 = one_hot(iota((L // 4, L), 1) // 4 == iota((L // 4, L), 0))
    quarter = dot(quarter, by4)
    half_x = ((iota((NA, L), 1) // 2) % 2).astype(f32)
    for z in range(HZ // 2):
        e = quarter[z * NA : (z + 1) * NA]
        w = quarter[(HZ // 2 + z) * NA : (HZ // 2 + z + 1) * NA] - half_x
        for dy in range(2):
            for dz in range(2):
                tile = jnp.where(w == 4.0 * dy + 2.0 * dz, e, 0.0).astype(bf16)
                row, col = (2 * z + dz + 1) * NA, (dy + 1) * L
                g2[row : row + NA, col : col + L] = tile

    by2 = one_hot(iota((L // 2, L), 1) // 2 == iota((L // 2, L), 0))
    halves = [first[:, y].astype(f32).reshape(NB * HZ, L // 2) for y in range(HY)]
    halves += [where_first[:, y].astype(f32).reshape(NB * HZ, L // 2) for y in range(HY)]
    halves = [dot(each.astype(bf16), by2).astype(bf16) for each in halves]
    r, s = iota((NB * HZ, NB * HZ), 0), iota((NB * HZ, NB * HZ), 1)
    order = one_hot(s == (r % NB) * HZ + r // NB)
    halves = dot(order, jnp.concatenate(halves, axis=1))
    pre1, p1 = halves[:, : HY * L], halves[:, HY * L :]
    slope1 = slope_of(pre1)
    act = jnp.where(pre1 > 0, pre1, LEAK * pre1).astype(bf16).astype(f32)

    pl.semaphore_wait(barrier, len(partners))

    def exchange(field, chans, ny, nz, base):
        copies = []
        rows = {-1: (0, chans), 0: (chans, nz * chans), 1: ((nz + 1) * chans, chans)}
        cols = {-1: (0, L), 0: (L, ny * L), 1: ((ny + 1) * L, L)}
        for index, (y, z) in enumerate(around):
            row, height = rows[-z]
            col, width = cols[-y]
            from_row = {-1: chans, 0: chans, 1: nz * chans}[z]
            from_col = {-1: L, 0: L, 1: ny * L}[y]
            copy = pltpu.make_async_remote_copy(
                src_ref=field.at[pl.ds(from_row, height), pl.ds(from_col, width)],
                dst_ref=field.at[pl.ds(row, height), pl.ds(col, width)],
                send_sem=sems.at[0, base + index],
                recv_sem=sems.at[1, base + index],
                device_id=device(y=y, z=z),
                device_id_type=MESH,
            )
            copy.start()
            copies.append(copy)
        return copies

    def clear_outside(field, chans, ny, nz):
        height, width = (nz + 2) * chans, (ny + 2) * L
        for on, row, col in (
            (gy == 0, slice(None), slice(0, L)),
            (gy == ngy - 1, slice(None), slice(width - L, width)),
            (gz == 0, slice(0, chans), slice(None)),
            (gz == ngz - 1, slice(height - chans, height), slice(None)),
        ):

            @pl.when(on)
            def _(row=row, col=col):
                field[row, col] = jnp.zeros_like(field[row, col])

    copies2 = exchange(g2, NA, HY, HZ, 0)

    tiled = dot(k2[...], one_hot(iota((NA, (HZ + 2) * NA), 1) % NA == iota((NA, (HZ + 2) * NA), 0)))
    z_of = iota((NB, (HZ + 2) * NA), 1) // NA
    for ty in range(3):
        for tx in range(3):
            for z in range(HZ):
                block = jnp.zeros((NB, (HZ + 2) * NA), f32)
                for tz in range(3):
                    t = ((ty * 3 + tz) * 3 + tx) * NB
                    block = jnp.where(z_of == z - tz + 2, tiled[t : t + NB], block)
                row = ((ty * 3 + tx) * HZ + z) * NB
                w2[row : row + NB, :] = block.astype(bf16)

    for y in range(HY):
        here = act[:, y * L : (y + 1) * L]
        for tx, by in enumerate((2, 0, -2)):
            value = (moved(here, by) if by else here).astype(bf16)
            for z in range(HZ):
                row = (z * 3 + tx) * NB
                a3[row : row + NB, y * L : (y + 1) * L] = value[z * NB : (z + 1) * NB]

    for copy in copies2:
        copy.wait()
    clear_outside(g2, NA, HY, HZ)

    rows2 = 3 * HZ * NB
    total = None
    for ty in range(3):
        part = dot(w2[ty * rows2 : (ty + 1) * rows2, :], g2[:, (2 - ty) * L : (2 - ty + HY) * L])
        total = part if total is None else total + part
    third = HZ * NB
    low = spread_across_x(total[:third], -2)
    high = spread_across_x(total[2 * third :], 2)
    odd_x = (iota((NB, L), 1) % 2).astype(f32)
    for y in range(HY):
        e = total[third : 2 * third, y * L : (y + 1) * L] + low[y] + high[y]
        e = e * slope1[:, y * L : (y + 1) * L]
        w = p1[:, y * L : (y + 1) * L]
        for z in range(HZ):
            ez = e[z * NB : (z + 1) * NB]
            wz = w[z * NB : (z + 1) * NB] - odd_x
            for dy in range(2):
                for dz in range(2):
                    row, col = (2 * z + dz + 1) * NB, (2 * y + dy + 1) * L
                    tile = jnp.where(wz == 4.0 * dy + 2.0 * dz, ez, 0.0).astype(bf16)
                    g1[row : row + NB, col : col + L] = tile

    copies1 = exchange(g1, NB, FY, FZ, 8)

    for ty in range(3):
        taps = None
        for z in range(HZ):
            part = dot_t(
                g2[z * NA : (z + 3) * NA, (2 - ty) * L : (2 - ty + HY) * L],
                a3[z * 3 * NB : (z + 1) * 3 * NB, :],
            )
            taps = part if taps is None else taps + part
        taps = taps * (0.5 * scales[1])
        for tz in range(3):
            row = (ty * 3 + tz) * NA
            s2[row : row + NA, :] = taps[(2 - tz) * NA : (3 - tz) * NA]

    for y in range(FY):
        for i in range(NC):
            here = vol[i, y].astype(f32)
            for tx, by in enumerate((1, 0, -1)):
                row = (tx * NC + i) * FZ
                v3[row : row + FZ, y * L : (y + 1) * L] = (
                    moved(here, by) if by else here
                ).astype(bf16)

    width = (FZ + 2) * NB
    tiled = dot(
        k1[...].astype(f32).reshape(27 * NC, NB).astype(bf16),
        one_hot(iota((NB, width), 1) % NB == iota((NB, width), 0)),
    )
    off = iota((FZ, width), 0) - iota((FZ, width), 1) // NB + 2
    for ty in range(3):
        for tx in range(3):
            for i in range(NC):
                block = jnp.zeros((FZ, width), f32)
                for tz in range(3):
                    t = ((ty * 3 + tz) * 3 + tx) * NC + i
                    line = jnp.broadcast_to(tiled[t : t + 1], (FZ, width))
                    block = jnp.where(off == tz, line, block)
                row = ((ty * 3 + tx) * NC + i) * FZ
                w1[row : row + FZ, :] = block.astype(bf16)

    for copy in copies1:
        copy.wait()
    clear_outside(g1, NB, FY, FZ)

    rows1 = 3 * NC * FZ
    z_of = iota((NB, rows1), 1) % FZ
    groups = jnp.where(iota((NC * 3, rows1), 1) // FZ == iota((NC * 3, rows1), 0), 1.0, 0.0)
    for ty in range(3):
        part = dot_t(g1[:, (2 - ty) * L : (2 - ty + FY) * L], v3[...])
        taps = []
        for tz in range(3):
            tap = jnp.zeros((NB, rows1), f32)
            for z in range(FZ + 2):
                if 0 <= z + tz - 2 < FZ:
                    tap = tap + jnp.where(z_of == z + tz - 2, part[z * NB : (z + 1) * NB], 0.0)
            taps.append(tap)
        taps = jnp.concatenate(taps, axis=0) * scales[0]
        s1[ty * 3 * NB : (ty + 1) * 3 * NB, :] = dot_t(
            taps, groups.astype(f32), lax.Precision.HIGHEST
        )

    msg[...] = jnp.zeros_like(msg)
    wide, per2, per1 = 3 * NB, NA // ndp, NB // ndp
    for k in range(ndp):
        for o in range(per2):
            msg[k, 0:9, o * wide : (o + 1) * wide] = s2[pl.ds(k * per2 + o, 9, stride=NA), :]
        for o in range(per1):
            at_lane = per2 * wide + o * 3 * NC
            msg[k, 0:9, at_lane : at_lane + 3 * NC] = s1[pl.ds(k * per1 + o, 9, stride=NB), :]

    copies_z = []
    for d in range(1, ndp):
        copy = pltpu.make_async_remote_copy(
            src_ref=msg.at[at(dp, d, ndp)],
            dst_ref=rz.at[d],
            send_sem=sem_z.at[0, d],
            recv_sem=sem_z.at[1, d],
            device_id=device(d=d),
            device_id_type=MESH,
        )
        copy.start()
        copies_z.append(copy)

    total = None
    for ty in range(3):
        part = dot(w1[ty * rows1 : (ty + 1) * rows1, :], g1[:, (2 - ty) * L : (2 - ty + FY) * L])
        total = part if total is None else total + part
    third = NC * FZ
    low = spread_across_x(total[:third], -1)
    high = spread_across_x(total[2 * third :], 1)
    for y in range(FY):
        value = total[third : 2 * third, y * L : (y + 1) * L] + low[y] + high[y]
        for i in range(NC):
            grad_vol[i, y] = value[i * FZ : (i + 1) * FZ].astype(bf16)

    for copy in copies_z:
        copy.wait()
    own = msg[dp]
    for d in range(1, ndp):
        own = own + rz[d]

    def shared(value, slots, sem, count, index, where):
        slots[index] = value
        copies = []
        for d in range(1, count):
            copy = pltpu.make_async_remote_copy(
                src_ref=slots.at[index],
                dst_ref=slots.at[index],
                send_sem=sem.at[0, d],
                recv_sem=sem.at[1, d],
                device_id=where(d),
                device_id_type=MESH,
            )
            copy.start()
            copies.append(copy)
        for copy in copies:
            copy.wait()
        value = slots[0]
        for d in range(1, count):
            value = value + slots[d]
        return value

    own = shared(own, ry, sem_y, ngy, gy, lambda d: device(y=d))
    out[...] = shared(own, rg, sem_g, ngz, gz, lambda d: device(z=d))


def shards(sizes, scales, volume, first, where_first, second, where_second, upstream, k1, k2):
    ndp, ngy, ngz = sizes
    k1 = jnp.transpose(k1, (2, 3, 4, 1, 0)).reshape(27, NC, NB)
    k2 = jnp.transpose(k2, (2, 3, 4, 1, 0)).reshape(27 * NB, NA)
    per2, per1 = NA // ndp, NB // ndp
    wide = pl.cdiv((per2 * NB + per1 * NC) * 3, L) * L
    vmem = pl.BlockSpec(memory_space=pltpu.VMEM)
    grad_vol, sums = pl.pallas_call(
        functools.partial(kernel, sizes, scales),
        out_shape=(
            jax.ShapeDtypeStruct((NC, FY, FZ, L), bf16),
            jax.ShapeDtypeStruct((16, wide), f32),
        ),
        in_specs=[vmem] * 8,
        out_specs=(vmem, vmem),
        scratch_shapes=[
            pltpu.VMEM(((HZ + 2) * NA, (HY + 2) * L), bf16),
            pltpu.VMEM(((FZ + 2) * NB, (FY + 2) * L), bf16),
            pltpu.VMEM((9 * HZ * NB, (HZ + 2) * NA), bf16),
            pltpu.VMEM((9 * NC * FZ, (FZ + 2) * NB), bf16),
            pltpu.VMEM((HZ * 3 * NB, HY * L), bf16),
            pltpu.VMEM((3 * NC * FZ, FY * L), bf16),
            pltpu.VMEM((9 * NA, 3 * NB), f32),
            pltpu.VMEM((9 * NB, 3 * NC), f32),
            pltpu.VMEM((ndp, 16, wide), f32),
            pltpu.VMEM((ndp, 16, wide), f32),
            pltpu.VMEM((ngy, 16, wide), f32),
            pltpu.VMEM((ngz, 16, wide), f32),
            pltpu.SemaphoreType.DMA((2, 16)),
            pltpu.SemaphoreType.DMA((2, ndp)),
            pltpu.SemaphoreType.DMA((2, ngy)),
            pltpu.SemaphoreType.DMA((2, ngz)),
        ],
        compiler_params=pltpu.CompilerParams(collective_id=0, has_side_effects=True),
    )(
        volume[0],
        first[0],
        where_first[0],
        second[0, :, 0],
        where_second[0, :, 0],
        upstream[0, :, 0],
        k1,
        k2,
    )
    sums = sums[:9]
    second_out = sums[:, : per2 * 3 * NB].reshape(3, 3, per2, 3, NB)
    second_out = jnp.transpose(second_out, (2, 4, 0, 1, 3)).reshape(-1)
    first_out = sums[:, per2 * 3 * NB : (per2 * NB + per1 * NC) * 3].reshape(3, 3, per1, 3, NC)
    first_out = jnp.transpose(first_out, (2, 4, 0, 1, 3)).reshape(-1)
    return (grad_vol[None], first_out, second_out)


def solution(mesh):
    sizes = tuple(mesh.shape[axis] for axis in ("dp", "gy", "gz"))
    cells = sizes[0] * sizes[1] * sizes[2] * FY * FZ * L
    scales = (math.sqrt(8.0 / cells), math.sqrt(64.0 / cells))
    split = P("dp", None, "gy", "gz", None)
    return jax.shard_map(
        functools.partial(shards, sizes, scales),
        mesh=mesh,
        in_specs=(split,) * 6 + (P(), P()),
        out_specs=(split, P("dp"), P("dp")),
        check_vma=False,
    )
```

```python
import functools
import math

import jax
import jax.numpy as jnp
from jax import lax
from jax.experimental import pallas as pl
from jax.experimental.pallas import tpu as pltpu
from jax.sharding import PartitionSpec as P

MESH = pl.DeviceIdType.MESH
f32, bf16, i32 = jnp.float32, jnp.bfloat16, jnp.int32
LEAK = 0.3
L = 128
NA, NB, NC = 32, 16, 4
HY, HZ = 2, 8
FY, FZ = 4, 16


def iota(shape, dim):
    return lax.broadcasted_iota(i32, shape, dim)


def dot(a, b):
    return lax.dot_general(a, b, (((1,), (0,)), ((), ())), preferred_element_type=f32)


def dot_t(a, b, precision=None):
    return lax.dot_general(
        a, b, (((1,), (1,)), ((), ())), preferred_element_type=f32, precision=precision
    )


def one_hot(mask):
    return jnp.where(mask, 1.0, 0.0).astype(bf16)


def slope_of(pre):
    return jnp.where(pre > 0, 1.0, LEAK).astype(f32)


def moved(value, by):
    lane = iota(value.shape, 1)
    inside = lane >= by if by > 0 else lane < L + by
    return jnp.where(inside, pltpu.roll(value, by % L, 1), 0.0)


def spread_across_x(value, by):
    return [moved(value[:, at : at + L], by) for at in range(0, value.shape[1], L)]


def exactly(value, mask):
    high = value.astype(bf16).astype(f32)
    middle = (value - high).astype(bf16).astype(f32)
    pieces = jnp.concatenate([high, middle, value - high - middle], axis=0).astype(bf16)
    pieces = dot(pieces, mask)
    rows = value.shape[0]
    return pieces[:rows] + pieces[rows : 2 * rows] + pieces[2 * rows :]


def kernel(
    sizes,
    scales,
    vol,
    first,
    where_first,
    second,
    where_second,
    upstream,
    k1,
    k2,
    grad_vol,
    out1,
    out2,
    g2,
    g1,
    w2,
    w1,
    a3,
    v3,
    vf,
    vh,
    s2,
    msg1,
    msg2,
    rz1,
    rz2,
    rp1,
    rp2,
    sem_h,
    sem_z,
    sem_p,
):
    ndp, ngy, ngz = sizes
    per2, per1 = NA // ndp, NB // ndp
    dp, gy, gz = lax.axis_index("dp"), lax.axis_index("gy"), lax.axis_index("gz")

    def at(index, step, count):
        return lax.rem(index + (step + count), count)

    def device(d=0, y=0, z=0):
        return {"dp": at(dp, d, ndp), "gy": at(gy, y, ngy), "gz": at(gz, z, ngz)}

    around = [(y, z) for y in (-1, 0, 1) for z in (-1, 0, 1) if (y, z) != (0, 0)]
    plane = [(y, z) for y in range(ngy) for z in range(ngz) if (y, z) != (0, 0)]

    def exists(y, z):
        on = None
        for step, index, count in ((y, gy, ngy), (z, gz, ngz)):
            if step:
                inside = index > 0 if step < 0 else index < count - 1
                on = inside if on is None else jnp.logical_and(on, inside)
        return on

    for field, chans, ny, nz in ((g2, NA, HY, HZ), (g1, NB, FY, FZ)):
        high, wide = (nz + 1) * chans, (ny + 1) * L
        for row, col in (
            (slice(0, chans), slice(None)),
            (slice(high, high + chans), slice(None)),
            (slice(chans, high), slice(0, L)),
            (slice(chans, high), slice(wide, wide + L)),
        ):
            field[row, col] = jnp.zeros_like(field[row, col])
    rows1 = 3 * NC * FZ
    v3[rows1:, :] = jnp.zeros_like(v3[rows1:, :])
    vh[...] = jnp.zeros_like(vh)
    s2[...] = jnp.zeros_like(s2)

    partners = [device(d=d) for d in range(1, ndp)] + [device(y=y, z=z) for y, z in plane]
    barrier = pltpu.get_barrier_semaphore()
    for one in partners:
        pl.semaphore_signal(barrier, inc=1, device_id=one, device_id_type=MESH)

    upf = upstream[...].astype(f32)
    e2 = (upf * slope_of(second[...].astype(f32))).astype(bf16).astype(f32)
    p2 = where_second[...].astype(f32)
    quarter = jnp.concatenate(
        [e2[:, z] for z in range(HZ // 2)] + [p2[:, z] for z in range(HZ // 2)], axis=0
    ).astype(bf16)
    by4 = one_hot(iota((L // 4, L), 1) // 4 == iota((L // 4, L), 0))
    quarter = dot(quarter, by4)
    half_x = ((iota((NA, L), 1) // 2) % 2).astype(f32)
    for z in range(HZ // 2):
        e = quarter[z * NA : (z + 1) * NA]
        w = quarter[(HZ // 2 + z) * NA : (HZ // 2 + z + 1) * NA] - half_x
        for dy in range(2):
            for dz in range(2):
                tile = jnp.where(w == 4.0 * dy + 2.0 * dz, e, 0.0).astype(bf16)
                row, col = (2 * z + dz + 1) * NA, (dy + 1) * L
                g2[row : row + NA, col : col + L] = tile

    def put_volume(here, i, col):
        for tx, by in enumerate((1, 0, -1)):
            row = (tx * NC + i) * FZ
            v3[row : row + FZ, col : col + L] = (moved(here, by) if by else here).astype(bf16)

    for y in range(FY):
        for i in range(NC):
            put_volume(vol[i, y].astype(f32), i, (y + 1) * L)
    r, c = iota((2 * NB, rows1), 0), iota((2 * NB, rows1), 1)
    sides = one_hot(c == (r % NB) * FZ + (r // NB) * (FZ - 1))
    vf[...] = dot(sides, v3[:rows1, L : (FY + 1) * L]).astype(bf16)

    by2 = one_hot(iota((L // 2, L), 1) // 2 == iota((L // 2, L), 0))
    halves = [first[:, y].astype(f32).reshape(NB * HZ, L // 2) for y in range(HY)]
    halves += [where_first[:, y].astype(f32).reshape(NB * HZ, L // 2) for y in range(HY)]
    halves = [dot(each.astype(bf16), by2).astype(bf16) for each in halves]
    r, c = iota((NB * HZ, NB * HZ), 0), iota((NB * HZ, NB * HZ), 1)
    order = one_hot(c == (r % NB) * HZ + r // NB)
    halves = dot(order, jnp.concatenate(halves, axis=1))
    pre1, p1 = halves[:, : HY * L], halves[:, HY * L :]
    slope1 = slope_of(pre1)
    act = jnp.where(pre1 > 0, pre1, LEAK * pre1).astype(bf16).astype(f32)

    pl.semaphore_wait(barrier, len(partners))

    def remote(src, dst, sems, index, to):
        return pltpu.make_async_remote_copy(
            src_ref=src,
            dst_ref=dst,
            send_sem=sems.at[0, index],
            recv_sem=sems.at[1, index],
            device_id=to,
            device_id_type=MESH,
        )

    def start(copies):
        for side, copy in copies:
            pl.when(exists(*side))(copy.start)

    def finish(copies):
        for (y, z), copy in copies:
            pl.when(exists(y, z))(copy.wait_send)
            pl.when(exists(-y, -z))(copy.wait_recv)

    def rim(field, chans, ny, nz, base):
        copies = []
        inner = {-1: (1, 1), 0: (1, None), 1: (None, 1)}
        for index, (y, z) in enumerate(around):
            height, width = (1 if z else nz), (1 if y else ny)
            from_row, to_row = (nz if z > 0 else 1), {-1: nz + 1, 0: 1, 1: 0}[z]
            from_col, to_col = (ny if y > 0 else 1), {-1: ny + 1, 0: 1, 1: 0}[y]
            source = field.at[
                pl.ds(from_row * chans, height * chans), pl.ds(from_col * L, width * L)
            ]
            target = field.at[
                pl.ds(to_row * chans, height * chans), pl.ds(to_col * L, width * L)
            ]
            copies.append(
                ((y, z), remote(source, target, sem_h, base + index, device(y=y, z=z)))
            )
        return copies

    def volume_rim(base):
        copies = []
        for index, (y, z) in enumerate(around):
            if z == 0:
                source, target = vol.at[:, FY - 1 if y > 0 else 0], vh.at[0 if y > 0 else 1]
            else:
                from_col, to_col = (FY - 1 if y > 0 else 0), {-1: FY + 1, 0: 1, 1: 0}[y]
                width = 1 if y else FY
                from_row, to_row = (NB if z > 0 else 0), rows1 + (0 if z > 0 else NB)
                source = vf.at[pl.ds(from_row, NB), pl.ds(from_col * L, width * L)]
                target = v3.at[pl.ds(to_row, NB), pl.ds(to_col * L, width * L)]
            copies.append(
                ((y, z), remote(source, target, sem_h, base + index, device(y=y, z=z)))
            )
        return copies

    rim2, rim_v = rim(g2, NA, HY, HZ, 0), volume_rim(8)
    start(rim2)
    start(rim_v)

    tiled = dot(k2[...], one_hot(iota((NA, (HZ + 2) * NA), 1) % NA == iota((NA, (HZ + 2) * NA), 0)))
    z_of = iota((NB, (HZ + 2) * NA), 1) // NA
    for ty in range(3):
        for tx in range(3):
            for z in range(HZ):
                block = jnp.zeros((NB, (HZ + 2) * NA), f32)
                for tz in range(3):
                    t = ((ty * 3 + tz) * 3 + tx) * NB
                    block = jnp.where(z_of == z - tz + 2, tiled[t : t + NB], block)
                row = ((ty * 3 + tx) * HZ + z) * NB
                w2[row : row + NB, :] = block.astype(bf16)

    for y in range(HY):
        here = act[:, y * L : (y + 1) * L]
        for tx, by in enumerate((2, 0, -2)):
            value = (moved(here, by) if by else here).astype(bf16)
            for z in range(HZ):
                row = (z * 3 + tx) * NB
                a3[row : row + NB, y * L : (y + 1) * L] = value[z * NB : (z + 1) * NB]

    width = (FZ + 2) * NB
    tiled = dot(
        k1[...].astype(f32).reshape(27 * NC, NB).astype(bf16),
        one_hot(iota((NB, width), 1) % NB == iota((NB, width), 0)),
    )
    off = iota((FZ, width), 0) - iota((FZ, width), 1) // NB + 2
    for ty in range(3):
        for tx in range(3):
            for i in range(NC):
                block = jnp.zeros((FZ, width), f32)
                for tz in range(3):
                    t = ((ty * 3 + tz) * 3 + tx) * NC + i
                    line = jnp.broadcast_to(tiled[t : t + 1], (FZ, width))
                    block = jnp.where(off == tz, line, block)
                row = ((ty * 3 + tx) * NC + i) * FZ
                w1[row : row + FZ, :] = block.astype(bf16)

    finish(rim2)

    for ty in range(3):
        taps = None
        for z in range(HZ):
            part = dot_t(
                g2[z * NA : (z + 3) * NA, (2 - ty) * L : (2 - ty + HY) * L],
                a3[z * 3 * NB : (z + 1) * 3 * NB, :],
            )
            taps = part if taps is None else taps + part
        taps = taps * (0.5 * scales[1])
        for tz in range(3):
            row = (ty * 3 + tz) * NA
            s2[row : row + NA, : 3 * NB] = taps[(2 - tz) * NA : (3 - tz) * NA]

    behind = per2 * 3 * NB
    def part_of_row(row, lane):
        value = s2[pl.ds(row, ndp, stride=per2), :]
        if msg2.shape[1] > L:
            rest = jnp.zeros((ndp, msg2.shape[1] - L), f32)
            value = jnp.concatenate([value, rest], axis=1)
        return pltpu.roll(value, lane, 1) if lane else value

    def masked(value, lane):
        at_lane = iota(value.shape, 1)
        return jnp.where(jnp.logical_and(at_lane >= lane, at_lane < lane + NB), value, 0.0)

    for tap in range(8):
        value = part_of_row(tap * NA, 0)
        for o in range(1, per2):
            value = value + part_of_row(tap * NA + o, o * 3 * NB)
        for piece in range(tap, 3 * per2, 8):
            lane, tx = behind + piece // 8 * NB, piece % 3
            moved_by = (lane - tx * NB) % msg2.shape[1]
            value = value + masked(part_of_row(8 * NA + piece // 3, moved_by), lane)
        msg2[pl.ds(tap, ndp, stride=8), :] = value

    def scatter(message, slots, base):
        copies = []
        for d in range(1, ndp):
            copy = remote(message(at(dp, d, ndp)), slots.at[d], sem_z, base + d, device(d=d))
            copy.start()
            copies.append(copy)
        return copies

    scatter2 = scatter(lambda k: msg2.at[pl.ds(pl.multiple_of(k * 8, 8), 8), :], rz2, 0)

    rows2 = 3 * HZ * NB
    total = None
    for ty in range(3):
        part = dot(w2[ty * rows2 : (ty + 1) * rows2, :], g2[:, (2 - ty) * L : (2 - ty + HY) * L])
        total = part if total is None else total + part
    third = HZ * NB
    low = spread_across_x(total[:third], -2)
    high = spread_across_x(total[2 * third :], 2)
    odd_x = (iota((NB, L), 1) % 2).astype(f32)
    for y in range(HY):
        e = total[third : 2 * third, y * L : (y + 1) * L] + low[y] + high[y]
        e = e * slope1[:, y * L : (y + 1) * L]
        w = p1[:, y * L : (y + 1) * L]
        for z in range(HZ):
            ez = e[z * NB : (z + 1) * NB]
            wz = w[z * NB : (z + 1) * NB] - odd_x
            for dy in range(2):
                for dz in range(2):
                    row, col = (2 * z + dz + 1) * NB, (2 * y + dy + 1) * L
                    tile = jnp.where(wz == 4.0 * dy + 2.0 * dz, ez, 0.0).astype(bf16)
                    g1[row : row + NB, col : col + L] = tile

    rim1 = rim(g1, NB, FY, FZ, 16)
    start(rim1)

    finish(rim_v)
    for side in range(2):
        for i in range(NC):
            put_volume(vh[side, i].astype(f32), i, side * (FY + 1) * L)

    count = rows1 + 2 * NB
    c = iota((NB, count), 1)
    z_of = jnp.where(c < rows1, c % FZ, jnp.where(c < rows1 + NB, -1, FZ))
    r, c = iota((count, L), 0), iota((count, L), 1)
    q = jnp.where(r < rows1, r // FZ, (r - rows1) % NB)
    lanes = one_hot(jnp.logical_and(q < 3 * NC, c == (q % NC) * 27 + q // NC))
    line = None
    for ty in range(3):
        part = dot_t(g1[NB : (FZ + 1) * NB, L : (FY + 1) * L], v3[:, ty * L : (ty + FY) * L])
        taps = []
        for tz in range(3):
            tap = None
            for z in range(FZ):
                add = jnp.where(z_of == z + tz - 1, part[z * NB : (z + 1) * NB], 0.0)
                tap = add if tap is None else tap + add
            taps.append(tap)
        taps = exactly(jnp.concatenate(taps, axis=0) * scales[0], lanes)
        for tz in range(3):
            tap = taps[tz * NB : (tz + 1) * NB]
            shift = (ty * 3 + tz) * 3
            tap = pltpu.roll(tap, shift, 1) if shift else tap
            line = tap if line is None else line + tap
    for k in range(ndp):
        for o in range(per1):
            row = k * per1 + o
            msg1[k, :, o * L : (o + 1) * L] = line[row : row + 1]

    scatter1 = scatter(lambda k: msg1.at[k], rz1, ndp)

    finish(rim1)

    total = None
    for ty in range(3):
        part = dot(w1[ty * rows1 : (ty + 1) * rows1, :], g1[:, (2 - ty) * L : (2 - ty + FY) * L])
        total = part if total is None else total + part
    third = NC * FZ
    low = spread_across_x(total[:third], -1)
    high = spread_across_x(total[2 * third :], 1)
    for y in range(FY):
        value = total[third : 2 * third, y * L : (y + 1) * L] + low[y] + high[y]
        for i in range(NC):
            grad_vol[i, y] = value[i * FZ : (i + 1) * FZ].astype(bf16)

    wide2 = pl.cdiv(out2.shape[0], L) * L
    r, c = iota((msg2.shape[1], wide2), 0), iota((msg2.shape[1], wide2), 1)
    of_row = (r // (3 * NB) * NB + r % NB) * 27 + r % (3 * NB) // NB
    to_main = one_hot(jnp.logical_and(r < behind, c == of_row))
    to_last = [
        one_hot(jnp.logical_and((r - behind) // NB == group, c == r % NB * 27))
        for group in range(pl.cdiv(3 * per2, 8))
    ]

    here = gy * ngz + gz

    def share(value, slots, base):
        slots[here] = value
        copies = []
        for index, (y, z) in enumerate(plane):
            copy = remote(slots.at[here], slots.at[here], sem_p, base + index, device(y=y, z=z))
            copy.start()
            copies.append(copy)
        return copies

    def gather(copies, slots):
        for copy in copies:
            copy.wait()
        value = slots[0]
        for d in range(1, ngy * ngz):
            value = value + slots[d]
        return value

    def reduce(copies, own, slots):
        for d, copy in enumerate(copies):
            copy.wait()
            own = own + slots[d + 1]
        return own

    own = msg2[pl.ds(pl.multiple_of(dp * 8, 8), 8), :]
    share2 = share(reduce(scatter2, own, rz2), rp2, 0)
    share1 = share(reduce(scatter1, msg1[dp], rz1), rp1, len(plane))

    sums = gather(share2, rp2)
    main = exactly(sums, to_main)
    line = None
    for tap in range(8):
        row = main[tap : tap + 1]
        row = pltpu.roll(row, 3 * tap, 1) if tap else row
        line = row if line is None else line + row
    last = [exactly(sums, lanes) for lanes in to_last]
    for piece in range(3 * per2):
        row = last[piece // 8][piece % 8 : piece % 8 + 1]
        line = line + pltpu.roll(row, piece // 3 * NB * 27 + 24 + piece % 3, 1)
    out2[...] = line[0, : out2.shape[0]]
    line = gather(share1, rp1)
    for o in range(per1):
        out1[o * NC * 27 : (o + 1) * NC * 27] = line[0, o * L : o * L + NC * 27]


def shards(sizes, scales, volume, first, where_first, second, where_second, upstream, k1, k2):
    ndp, ngy, ngz = sizes
    k1 = jnp.transpose(k1, (2, 3, 4, 1, 0)).reshape(27, NC, NB)
    k2 = jnp.transpose(k2, (2, 3, 4, 1, 0)).reshape(27 * NB, NA)
    per2, per1 = NA // ndp, NB // ndp
    wide1 = per1 * L
    wide2 = pl.cdiv(per2 * 3 * NB + pl.cdiv(3 * per2, 8) * NB, L) * L
    there = ngy * ngz
    vmem = pl.BlockSpec(memory_space=pltpu.VMEM)
    grad_vol, first_out, second_out = pl.pallas_call(
        functools.partial(kernel, sizes, scales),
        out_shape=(
            jax.ShapeDtypeStruct((NC, FY, FZ, L), bf16),
            jax.ShapeDtypeStruct((per1 * NC * 27,), f32),
            jax.ShapeDtypeStruct((per2 * NB * 27,), f32),
        ),
        in_specs=[vmem] * 8,
        out_specs=(vmem,) * 3,
        scratch_shapes=[
            pltpu.VMEM(((HZ + 2) * NA, (HY + 2) * L), bf16),
            pltpu.VMEM(((FZ + 2) * NB, (FY + 2) * L), bf16),
            pltpu.VMEM((9 * HZ * NB, (HZ + 2) * NA), bf16),
            pltpu.VMEM((9 * NC * FZ, (FZ + 2) * NB), bf16),
            pltpu.VMEM((HZ * 3 * NB, HY * L), bf16),
            pltpu.VMEM((3 * NC * FZ + 2 * NB, (FY + 2) * L), bf16),
            pltpu.VMEM((2 * NB, FY * L), bf16),
            pltpu.VMEM((2, NC, FZ, L), bf16),
            pltpu.VMEM((9 * NA, L), f32),
            pltpu.VMEM((ndp, 1, wide1), f32),
            pltpu.VMEM((ndp * 8, wide2), f32),
            pltpu.VMEM((ndp, 1, wide1), f32),
            pltpu.VMEM((ndp, 8, wide2), f32),
            pltpu.VMEM((there, 1, wide1), f32),
            pltpu.VMEM((there, 8, wide2), f32),
            pltpu.SemaphoreType.DMA((2, 24)),
            pltpu.SemaphoreType.DMA((2, 2 * ndp)),
            pltpu.SemaphoreType.DMA((2, 2 * there)),
        ],
        compiler_params=pltpu.CompilerParams(collective_id=0, has_side_effects=True),
    )(
        volume[0],
        first[0],
        where_first[0],
        second[0, :, 0],
        where_second[0, :, 0],
        upstream[0, :, 0],
        k1,
        k2,
    )
    return (grad_vol[None], first_out, second_out)


def solution(mesh):
    sizes = tuple(mesh.shape[axis] for axis in ("dp", "gy", "gz"))
    cells = sizes[0] * sizes[1] * sizes[2] * FY * FZ * L
    scales = (math.sqrt(8.0 / cells), math.sqrt(64.0 / cells))
    split = P("dp", None, "gy", "gz", None)
    return jax.shard_map(
        functools.partial(shards, sizes, scales),
        mesh=mesh,
        in_specs=(split,) * 6 + (P(), P()),
        out_specs=(split, P("dp"), P("dp")),
        check_vma=False,
    )
```

```python
import functools
import math

import jax
import jax.numpy as jnp
from jax import lax
from jax.experimental import pallas as pl
from jax.experimental.pallas import tpu as pltpu
from jax.sharding import PartitionSpec as P

MESH = pl.DeviceIdType.MESH
f32, bf16, i32 = jnp.float32, jnp.bfloat16, jnp.int32
LEAK = 0.3
L = 128
NA, NB, NC = 32, 16, 4
HY, HZ = 2, 8
FY, FZ = 4, 16


def iota(shape, dim):
    return lax.broadcasted_iota(i32, shape, dim)


def dot(a, b):
    return lax.dot_general(a, b, (((1,), (0,)), ((), ())), preferred_element_type=f32)


def dot_t(a, b, precision=None):
    return lax.dot_general(
        a, b, (((1,), (1,)), ((), ())), preferred_element_type=f32, precision=precision
    )


def one_hot(mask):
    return jnp.where(mask, 1.0, 0.0).astype(bf16)


def slope_of(pre):
    return jnp.where(pre > 0, 1.0, LEAK).astype(f32)


def moved(value, by):
    lane = iota(value.shape, 1)
    inside = lane >= by if by > 0 else lane < L + by
    return jnp.where(inside, pltpu.roll(value, by % L, 1), 0.0)


def spread_across_x(value, by):
    return [moved(value[:, at : at + L], by) for at in range(0, value.shape[1], L)]


def exactly(value, mask):
    high = value.astype(bf16).astype(f32)
    middle = (value - high).astype(bf16).astype(f32)
    pieces = jnp.concatenate([high, middle, value - high - middle], axis=0).astype(bf16)
    pieces = dot(pieces, mask)
    rows = value.shape[0]
    return pieces[:rows] + pieces[rows : 2 * rows] + pieces[2 * rows :]


def kernel(
    sizes,
    scales,
    vol,
    first,
    where_first,
    second,
    where_second,
    upstream,
    k1,
    k2,
    grad_vol,
    out1,
    out2,
    g2,
    g1,
    w2,
    w1,
    a3,
    v3,
    vf,
    vh,
    vz,
    py,
    pz,
    qy,
    qz,
    s2,
    msg1,
    msg2,
    rz1,
    rz2,
    rp1,
    rp2,
    sem_h,
    sem_z,
    sem_p,
    sem_r,
):
    ndp, ngy, ngz = sizes
    per2, per1 = NA // ndp, NB // ndp
    dp, gy, gz = lax.axis_index("dp"), lax.axis_index("gy"), lax.axis_index("gz")

    def at(index, step, count):
        return lax.rem(index + (step + count), count)

    def device(d=0, y=0, z=0):
        return {"dp": at(dp, d, ndp), "gy": at(gy, y, ngy), "gz": at(gz, z, ngz)}

    around = [(y, z) for y in (-1, 0, 1) for z in (-1, 0, 1) if (y, z) != (0, 0)]
    plane = [(y, z) for y in range(ngy) for z in range(ngz) if (y, z) != (0, 0)]

    def exists(y, z):
        on = None
        for step, index, count in ((y, gy, ngy), (z, gz, ngz)):
            if step:
                inside = index > 0 if step < 0 else index < count - 1
                on = inside if on is None else jnp.logical_and(on, inside)
        return on

    for field, chans, ny, nz in ((g2, NA, HY, HZ), (g1, NB, FY, FZ)):
        high, wide = (nz + 1) * chans, (ny + 1) * L
        for row, col in (
            (slice(0, chans), slice(None)),
            (slice(high, high + chans), slice(None)),
            (slice(chans, high), slice(0, L)),
            (slice(chans, high), slice(wide, wide + L)),
        ):
            field[row, col] = jnp.zeros_like(field[row, col])
    rows1 = 3 * NC * FZ
    for field in (vh, vz, qy, qz):
        field[...] = jnp.zeros_like(field)
    s2[...] = jnp.zeros_like(s2)

    partners = [dict(y=y, z=z) for y, z in around] + [dict(d=1), dict(d=-1)]
    heard = [partners]
    for step in range(1, rounds_of(sizes)):
        far = []
        for axis, count in (("d", ndp), ("y", ngy), ("z", ngz)):
            if 2**step < count // 2:
                far += [{axis: 2**step}, {axis: -(2**step)}]
        heard.append(far)
    partners = [device(**one) for one in partners]
    barrier = pltpu.get_barrier_semaphore()
    for one in partners:
        pl.semaphore_signal(barrier, inc=1, device_id=one, device_id_type=MESH)

    upf = upstream[...].astype(f32)
    e2 = (upf * slope_of(second[...].astype(f32))).astype(bf16).astype(f32)
    p2 = where_second[...].astype(f32)
    quarter = jnp.concatenate(
        [e2[:, z] for z in range(HZ // 2)] + [p2[:, z] for z in range(HZ // 2)], axis=0
    ).astype(bf16)
    by4 = one_hot(iota((L // 4, L), 1) // 4 == iota((L // 4, L), 0))
    quarter = dot(quarter, by4)
    half_x = ((iota((NA, L), 1) // 2) % 2).astype(f32)
    odd = iota((NA, L), 1) % 2 == 1
    tiles = {}
    for z in range(HZ // 2):
        e = quarter[z * NA : (z + 1) * NA]
        w = quarter[(HZ // 2 + z) * NA : (HZ // 2 + z + 1) * NA] - half_x
        for dy in range(2):
            for dz in range(2):
                tile = jnp.where(w == 4.0 * dy + 2.0 * dz, e, 0.0)
                row, col = (2 * z + dz + 1) * NA, (dy + 1) * L
                g2[row : row + NA, col : col + L] = tile.astype(bf16)
                tiles[2 * z + dz, dy] = tile
    for side, at_y, at_z in ((0, 0, 0), (1, HY - 1, HZ - 1)):
        for z in range(HZ // 2):
            pair = jnp.where(odd, tiles[2 * z + 1, at_y], tiles[2 * z, at_y])
            py[side, z * NA : (z + 1) * NA] = pair.astype(bf16)
        pz[side] = jnp.where(odd, tiles[at_z, 1], tiles[at_z, 0]).astype(bf16)

    def unpaired(value):
        value = value.astype(f32)
        even_half = jnp.where(odd, pltpu.roll(value, 1, 1), value)
        odd_half = jnp.where(odd, value, pltpu.roll(value, L - 1, 1))
        return even_half.astype(bf16), odd_half.astype(bf16)

    def put_volume(here, i, col):
        for tx, by in enumerate((1, 0, -1)):
            row = (tx * NC + i) * FZ
            v3[row : row + FZ, col : col + L] = (moved(here, by) if by else here).astype(bf16)

    for y in range(FY):
        value = vol[:, y].astype(f32)
        vf[0, y] = value[:, 0].astype(bf16)
        vf[1, y] = value[:, FZ - 1].astype(bf16)
        for i in range(NC):
            put_volume(value[i], i, (y + 1) * L)

    by2 = one_hot(iota((L // 2, L), 1) // 2 == iota((L // 2, L), 0))
    halves = [first[:, y].astype(f32).reshape(NB * HZ, L // 2) for y in range(HY)]
    halves += [where_first[:, y].astype(f32).reshape(NB * HZ, L // 2) for y in range(HY)]
    halves = [dot(each.astype(bf16), by2).astype(bf16) for each in halves]
    r, c = iota((NB * HZ, NB * HZ), 0), iota((NB * HZ, NB * HZ), 1)
    order = one_hot(c == (r % NB) * HZ + r // NB)
    halves = dot(order, jnp.concatenate(halves, axis=1))
    pre1, p1 = halves[:, : HY * L], halves[:, HY * L :]
    slope1 = slope_of(pre1)
    act = jnp.where(pre1 > 0, pre1, LEAK * pre1).astype(bf16).astype(f32)

    pl.semaphore_wait(barrier, len(partners))

    def remote(src, dst, sems, index, to):
        return pltpu.make_async_remote_copy(
            src_ref=src,
            dst_ref=dst,
            send_sem=sems.at[0, index],
            recv_sem=sems.at[1, index],
            device_id=to,
            device_id_type=MESH,
        )

    def start(copies):
        for side, copy in copies:
            pl.when(exists(*side))(copy.start)

    def finish(copies):
        for (y, z), copy in copies:
            pl.when(exists(y, z))(copy.wait_send)
            pl.when(exists(-y, -z))(copy.wait_recv)

    def rim(field, chans, ny, nz, base):
        copies = []
        for index, (y, z) in enumerate(around):
            height, width = (1 if z else nz), (1 if y else ny)
            from_row, to_row = (nz if z > 0 else 1), {-1: nz + 1, 0: 1, 1: 0}[z]
            from_col, to_col = (ny if y > 0 else 1), {-1: ny + 1, 0: 1, 1: 0}[y]
            source = field.at[
                pl.ds(from_row * chans, height * chans), pl.ds(from_col * L, width * L)
            ]
            target = field.at[
                pl.ds(to_row * chans, height * chans), pl.ds(to_col * L, width * L)
            ]
            copies.append(
                ((y, z), remote(source, target, sem_h, base + index, device(y=y, z=z)))
            )
        return copies

    def volume_rim(base):
        copies = []
        for index, (y, z) in enumerate(around):
            if z == 0:
                source, target = vol.at[:, FY - 1 if y > 0 else 0], vh.at[0 if y > 0 else 1]
            else:
                from_y, to_y = (FY - 1 if y > 0 else 0), {-1: FY + 1, 0: 1, 1: 0}[y]
                width = 1 if y else FY
                source = vf.at[1 if z > 0 else 0, pl.ds(from_y, width)]
                target = vz.at[0 if z > 0 else 1, pl.ds(to_y, width)]
            copies.append(
                ((y, z), remote(source, target, sem_h, base + index, device(y=y, z=z)))
            )
        return copies

    def paired_rim(base):
        copies = []
        for index, (y, z) in enumerate(around):
            if y and z:
                row, to_row = (HZ if z > 0 else 1), (0 if z > 0 else HZ + 1)
                col, to_col = (HY if y > 0 else 1), (0 if y > 0 else HY + 1)
                source = g2.at[pl.ds(row * NA, NA), pl.ds(col * L, L)]
                target = g2.at[pl.ds(to_row * NA, NA), pl.ds(to_col * L, L)]
            else:
                up = 1 if y + z > 0 else 0
                source, target = (py.at[up], qy.at[1 - up]) if y else (pz.at[up], qz.at[1 - up])
            copies.append(
                ((y, z), remote(source, target, sem_h, base + index, device(y=y, z=z)))
            )
        return copies

    rim2, rim_v = paired_rim(0), volume_rim(8)
    start(rim2)
    start(rim_v)

    def announce(step):
        for one in heard[step]:
            pl.semaphore_signal(
                sem_r.at[step], inc=1, device_id=device(**one), device_id_type=MESH
            )

    announce(0)

    tiled = dot(k2[...], one_hot(iota((NA, (HZ + 2) * NA), 1) % NA == iota((NA, (HZ + 2) * NA), 0)))
    z_of = iota((NB, (HZ + 2) * NA), 1) // NA
    for ty in range(3):
        for tx in range(3):
            for z in range(HZ):
                block = jnp.zeros((NB, (HZ + 2) * NA), f32)
                for tz in range(3):
                    t = ((ty * 3 + tz) * 3 + tx) * NB
                    block = jnp.where(z_of == z - tz + 2, tiled[t : t + NB], block)
                row = ((ty * 3 + tx) * HZ + z) * NB
                w2[row : row + NB, :] = block.astype(bf16)

    for y in range(HY):
        here = act[:, y * L : (y + 1) * L]
        for tx, by in enumerate((2, 0, -2)):
            value = (moved(here, by) if by else here).astype(bf16)
            for z in range(HZ):
                row = (z * 3 + tx) * NB
                a3[row : row + NB, y * L : (y + 1) * L] = value[z * NB : (z + 1) * NB]

    width = (FZ + 2) * NB
    tiled = dot(
        k1[...].astype(f32).reshape(27 * NC, NB).astype(bf16),
        one_hot(iota((NB, width), 1) % NB == iota((NB, width), 0)),
    )
    off = iota((FZ, width), 0) - iota((FZ, width), 1) // NB + 2
    for ty in range(3):
        for tx in range(3):
            for i in range(NC):
                block = jnp.zeros((FZ, width), f32)
                for tz in range(3):
                    t = ((ty * 3 + tz) * 3 + tx) * NC + i
                    line = jnp.broadcast_to(tiled[t : t + 1], (FZ, width))
                    block = jnp.where(off == tz, line, block)
                row = ((ty * 3 + tx) * NC + i) * FZ
                w1[row : row + FZ, :] = block.astype(bf16)

    for step in range(len(heard)):
        pl.semaphore_wait(sem_r.at[step], len(heard[step]))
        if step + 1 < len(heard):
            announce(step + 1)

    finish(rim2)
    for side in range(2):
        row, col = side * (HZ + 1) * NA, side * (HY + 1) * L
        g2[row : row + NA, L : 2 * L], g2[row : row + NA, 2 * L : 3 * L] = unpaired(qz[side])
        for z in range(HZ // 2):
            low, high = unpaired(qy[side, z * NA : (z + 1) * NA])
            row = (2 * z + 1) * NA
            g2[row : row + NA, col : col + L] = low
            g2[row + NA : row + 2 * NA, col : col + L] = high

    for ty in range(3):
        taps = None
        for z in range(HZ):
            part = dot_t(
                g2[z * NA : (z + 3) * NA, (2 - ty) * L : (2 - ty + HY) * L],
                a3[z * 3 * NB : (z + 1) * 3 * NB, :],
            )
            taps = part if taps is None else taps + part
        taps = taps * (0.5 * scales[1])
        for tz in range(3):
            row = (ty * 3 + tz) * NA
            s2[row : row + NA, : 3 * NB] = taps[(2 - tz) * NA : (3 - tz) * NA]

    behind = per2 * 3 * NB
    def part_of_row(row, lane):
        value = s2[pl.ds(row, ndp, stride=per2), :]
        if msg2.shape[1] > L:
            rest = jnp.zeros((ndp, msg2.shape[1] - L), f32)
            value = jnp.concatenate([value, rest], axis=1)
        return pltpu.roll(value, lane, 1) if lane else value

    def masked(value, lane):
        at_lane = iota(value.shape, 1)
        return jnp.where(jnp.logical_and(at_lane >= lane, at_lane < lane + NB), value, 0.0)

    for tap in range(8):
        value = part_of_row(tap * NA, 0)
        for o in range(1, per2):
            value = value + part_of_row(tap * NA + o, o * 3 * NB)
        for piece in range(tap, 3 * per2, 8):
            lane, tx = behind + piece // 8 * NB, piece % 3
            moved_by = (lane - tx * NB) % msg2.shape[1]
            value = value + masked(part_of_row(8 * NA + piece // 3, moved_by), lane)
        msg2[pl.ds(tap, ndp, stride=8), :] = value

    def scatter(message, slots, base):
        copies = []
        for d in range(1, ndp):
            copy = remote(message(at(dp, d, ndp)), slots.at[d], sem_z, base + d, device(d=d))
            copy.start()
            copies.append(copy)
        return copies

    scatter2 = scatter(lambda k: msg2.at[pl.ds(pl.multiple_of(k * 8, 8), 8), :], rz2, 0)

    rows2 = 3 * HZ * NB
    total = None
    for ty in range(3):
        part = dot(w2[ty * rows2 : (ty + 1) * rows2, :], g2[:, (2 - ty) * L : (2 - ty + HY) * L])
        total = part if total is None else total + part
    third = HZ * NB
    low = spread_across_x(total[:third], -2)
    high = spread_across_x(total[2 * third :], 2)
    odd_x = (iota((NB, L), 1) % 2).astype(f32)
    for y in range(HY):
        e = total[third : 2 * third, y * L : (y + 1) * L] + low[y] + high[y]
        e = e * slope1[:, y * L : (y + 1) * L]
        w = p1[:, y * L : (y + 1) * L]
        for z in range(HZ):
            ez = e[z * NB : (z + 1) * NB]
            wz = w[z * NB : (z + 1) * NB] - odd_x
            for dy in range(2):
                for dz in range(2):
                    row, col = (2 * z + dz + 1) * NB, (2 * y + dy + 1) * L
                    tile = jnp.where(wz == 4.0 * dy + 2.0 * dz, ez, 0.0).astype(bf16)
                    g1[row : row + NB, col : col + L] = tile

    rim1 = rim(g1, NB, FY, FZ, 16)
    start(rim1)

    finish(rim_v)
    for side in range(2):
        for i in range(NC):
            put_volume(vh[side, i].astype(f32), i, side * (FY + 1) * L)
        for y in range(FY + 2):
            here = vz[side, y].astype(f32)
            layers = [moved(here, 1), here, moved(here, -1), jnp.zeros_like(here)]
            row = rows1 + side * NB
            v3[row : row + NB, y * L : (y + 1) * L] = jnp.concatenate(layers, axis=0).astype(bf16)

    count = rows1 + 2 * NB
    c = iota((NB, count), 1)
    z_of = jnp.where(c < rows1, c % FZ, jnp.where(c < rows1 + NB, -1, FZ))
    r, c = iota((count, L), 0), iota((count, L), 1)
    q = jnp.where(r < rows1, r // FZ, (r - rows1) % NB)
    lanes = one_hot(jnp.logical_and(q < 3 * NC, c == (q % NC) * 27 + q // NC))
    line = None
    for ty in range(3):
        part = dot_t(g1[NB : (FZ + 1) * NB, L : (FY + 1) * L], v3[:, ty * L : (ty + FY) * L])
        taps = []
        for tz in range(3):
            tap = None
            for z in range(FZ):
                add = jnp.where(z_of == z + tz - 1, part[z * NB : (z + 1) * NB], 0.0)
                tap = add if tap is None else tap + add
            taps.append(tap)
        taps = exactly(jnp.concatenate(taps, axis=0) * scales[0], lanes)
        for tz in range(3):
            tap = taps[tz * NB : (tz + 1) * NB]
            shift = (ty * 3 + tz) * 3
            tap = pltpu.roll(tap, shift, 1) if shift else tap
            line = tap if line is None else line + tap
    for k in range(ndp):
        for o in range(per1):
            row = k * per1 + o
            msg1[k, :, o * L : (o + 1) * L] = line[row : row + 1]

    scatter1 = scatter(lambda k: msg1.at[k], rz1, ndp)

    finish(rim1)

    total = None
    for ty in range(3):
        part = dot(w1[ty * rows1 : (ty + 1) * rows1, :], g1[:, (2 - ty) * L : (2 - ty + FY) * L])
        total = part if total is None else total + part
    third = NC * FZ
    low = spread_across_x(total[:third], -1)
    high = spread_across_x(total[2 * third :], 1)
    for y in range(FY):
        value = total[third : 2 * third, y * L : (y + 1) * L] + low[y] + high[y]
        for i in range(NC):
            grad_vol[i, y] = value[i * FZ : (i + 1) * FZ].astype(bf16)

    wide2 = pl.cdiv(out2.shape[0], L) * L
    r, c = iota((msg2.shape[1], wide2), 0), iota((msg2.shape[1], wide2), 1)
    of_row = (r // (3 * NB) * NB + r % NB) * 27 + r % (3 * NB) // NB
    to_main = one_hot(jnp.logical_and(r < behind, c == of_row))
    to_last = [
        one_hot(jnp.logical_and((r - behind) // NB == group, c == r % NB * 27))
        for group in range(pl.cdiv(3 * per2, 8))
    ]

    here = gy * ngz + gz

    def share(value, slots, base):
        slots[here] = value
        copies = []
        for index, (y, z) in enumerate(plane):
            copy = remote(slots.at[here], slots.at[here], sem_p, base + index, device(y=y, z=z))
            copy.start()
            copies.append(copy)
        return copies

    def gather(copies, slots):
        for copy in copies:
            copy.wait()
        value = slots[0]
        for d in range(1, ngy * ngz):
            value = value + slots[d]
        return value

    def reduce(copies, own, slots):
        for d, copy in enumerate(copies):
            copy.wait()
            own = own + slots[d + 1]
        return own

    own = msg2[pl.ds(pl.multiple_of(dp * 8, 8), 8), :]
    share2 = share(reduce(scatter2, own, rz2), rp2, 0)
    share1 = share(reduce(scatter1, msg1[dp], rz1), rp1, len(plane))

    sums = gather(share2, rp2)
    main = exactly(sums, to_main)
    line = None
    for tap in range(8):
        row = main[tap : tap + 1]
        row = pltpu.roll(row, 3 * tap, 1) if tap else row
        line = row if line is None else line + row
    last = [exactly(sums, lanes) for lanes in to_last]
    for piece in range(3 * per2):
        row = last[piece // 8][piece % 8 : piece % 8 + 1]
        line = line + pltpu.roll(row, piece // 3 * NB * 27 + 24 + piece % 3, 1)
    out2[...] = line[0, : out2.shape[0]]
    line = gather(share1, rp1)
    for o in range(per1):
        out1[o * NC * 27 : (o + 1) * NC * 27] = line[0, o * L : o * L + NC * 27]


def rounds_of(sizes):
    return max(1, (max(sizes) // 2 - 1).bit_length())


def shards(sizes, scales, volume, first, where_first, second, where_second, upstream, k1, k2):
    ndp, ngy, ngz = sizes
    k1 = jnp.transpose(k1, (2, 3, 4, 1, 0)).reshape(27, NC, NB)
    k2 = jnp.transpose(k2, (2, 3, 4, 1, 0)).reshape(27 * NB, NA)
    per2, per1 = NA // ndp, NB // ndp
    wide1 = per1 * L
    wide2 = pl.cdiv(per2 * 3 * NB + pl.cdiv(3 * per2, 8) * NB, L) * L
    there = ngy * ngz
    vmem = pl.BlockSpec(memory_space=pltpu.VMEM)
    grad_vol, first_out, second_out = pl.pallas_call(
        functools.partial(kernel, sizes, scales),
        out_shape=(
            jax.ShapeDtypeStruct((NC, FY, FZ, L), bf16),
            jax.ShapeDtypeStruct((per1 * NC * 27,), f32),
            jax.ShapeDtypeStruct((per2 * NB * 27,), f32),
        ),
        in_specs=[vmem] * 8,
        out_specs=(vmem,) * 3,
        scratch_shapes=[
            pltpu.VMEM(((HZ + 2) * NA, (HY + 2) * L), bf16),
            pltpu.VMEM(((FZ + 2) * NB, (FY + 2) * L), bf16),
            pltpu.VMEM((9 * HZ * NB, (HZ + 2) * NA), bf16),
            pltpu.VMEM((9 * NC * FZ, (FZ + 2) * NB), bf16),
            pltpu.VMEM((HZ * 3 * NB, HY * L), bf16),
            pltpu.VMEM((3 * NC * FZ + 2 * NB, (FY + 2) * L), bf16),
            pltpu.VMEM((2, FY, NC, L), bf16),
            pltpu.VMEM((2, NC, FZ, L), bf16),
            pltpu.VMEM((2, FY + 2, NC, L), bf16),
            pltpu.VMEM((2, HZ // 2 * NA, L), bf16),
            pltpu.VMEM((2, NA, L), bf16),
            pltpu.VMEM((2, HZ // 2 * NA, L), bf16),
            pltpu.VMEM((2, NA, L), bf16),
            pltpu.VMEM((9 * NA, L), f32),
            pltpu.VMEM((ndp, 1, wide1), f32),
            pltpu.VMEM((ndp * 8, wide2), f32),
            pltpu.VMEM((ndp, 1, wide1), f32),
            pltpu.VMEM((ndp, 8, wide2), f32),
            pltpu.VMEM((there, 1, wide1), f32),
            pltpu.VMEM((there, 8, wide2), f32),
            pltpu.SemaphoreType.DMA((2, 24)),
            pltpu.SemaphoreType.DMA((2, 2 * ndp)),
            pltpu.SemaphoreType.DMA((2, 2 * there)),
            pltpu.SemaphoreType.REGULAR((rounds_of(sizes),)),
        ],
        compiler_params=pltpu.CompilerParams(collective_id=0, has_side_effects=True),
    )(
        volume[0],
        first[0],
        where_first[0],
        second[0, :, 0],
        where_second[0, :, 0],
        upstream[0, :, 0],
        k1,
        k2,
    )
    return (grad_vol[None], first_out, second_out)


def solution(mesh):
    sizes = tuple(mesh.shape[axis] for axis in ("dp", "gy", "gz"))
    cells = sizes[0] * sizes[1] * sizes[2] * FY * FZ * L
    scales = (math.sqrt(8.0 / cells), math.sqrt(64.0 / cells))
    split = P("dp", None, "gy", "gz", None)
    return jax.shard_map(
        functools.partial(shards, sizes, scales),
        mesh=mesh,
        in_specs=(split,) * 6 + (P(), P()),
        out_specs=(split, P("dp"), P("dp")),
        check_vma=False,
    )
```

```python
import functools
import math

import jax
import jax.numpy as jnp
from jax import lax
from jax.experimental import pallas as pl
from jax.experimental.pallas import tpu as pltpu
from jax.sharding import PartitionSpec as P

MESH = pl.DeviceIdType.MESH
f32, bf16, i32 = jnp.float32, jnp.bfloat16, jnp.int32
LEAK = 0.3
L = 128
NA, NB, NC = 32, 16, 4
HY, HZ = 2, 8
FY, FZ = 4, 16


def iota(shape, dim):
    return lax.broadcasted_iota(i32, shape, dim)


def dot(a, b):
    return lax.dot_general(a, b, (((1,), (0,)), ((), ())), preferred_element_type=f32)


def dot_t(a, b, precision=None):
    return lax.dot_general(
        a, b, (((1,), (1,)), ((), ())), preferred_element_type=f32, precision=precision
    )


def one_hot(mask):
    return jnp.where(mask, 1.0, 0.0).astype(bf16)


def slope_of(pre):
    return jnp.where(pre > 0, 1.0, LEAK).astype(f32)


def moved(value, by):
    lane = iota(value.shape, 1)
    inside = lane >= by if by > 0 else lane < L + by
    return jnp.where(inside, pltpu.roll(value, by % L, 1), 0.0)


def spread_across_x(value, by):
    return [moved(value[:, at : at + L], by) for at in range(0, value.shape[1], L)]


def exactly(value, mask):
    high = value.astype(bf16).astype(f32)
    middle = (value - high).astype(bf16).astype(f32)
    pieces = jnp.concatenate([high, middle, value - high - middle], axis=0).astype(bf16)
    pieces = dot(pieces, mask)
    rows = value.shape[0]
    return pieces[:rows] + pieces[rows : 2 * rows] + pieces[2 * rows :]


def kernel(
    sizes,
    scales,
    *refs,
):
    arguments, refs = refs[:8], refs[8:]
    copied, refs = refs[-9:-1], refs[:-9] + refs[-1:]
    loads = [
        pltpu.make_async_copy(source, target, refs[-1].at[index])
        for index, (source, target) in enumerate(zip(arguments, copied))
    ]
    for load in loads:
        load.start()
    body(sizes, scales, loads, *copied, *refs[:-1])


def body(
    sizes,
    scales,
    loads,
    vol,
    first,
    where_first,
    second,
    where_second,
    upstream,
    k1,
    k2,
    grad_vol,
    out1,
    out2,
    g2,
    g1,
    w2,
    w1,
    a3,
    v3,
    vf,
    vh,
    vz,
    py,
    pz,
    qy,
    qz,
    s2,
    msg1,
    msg2,
    rz1,
    rz2,
    rp1,
    rp2,
    sem_h,
    sem_z,
    sem_p,
    sem_r,
):
    ndp, ngy, ngz = sizes
    per2, per1 = NA // ndp, NB // ndp
    dp, gy, gz = lax.axis_index("dp"), lax.axis_index("gy"), lax.axis_index("gz")

    def at(index, step, count):
        return lax.rem(index + (step + count), count)

    def device(d=0, y=0, z=0):
        return {"dp": at(dp, d, ndp), "gy": at(gy, y, ngy), "gz": at(gz, z, ngz)}

    around = [(y, z) for y in (-1, 0, 1) for z in (-1, 0, 1) if (y, z) != (0, 0)]
    plane = [(y, z) for y in range(ngy) for z in range(ngz) if (y, z) != (0, 0)]

    def exists(y, z):
        on = None
        for step, index, count in ((y, gy, ngy), (z, gz, ngz)):
            if step:
                inside = index > 0 if step < 0 else index < count - 1
                on = inside if on is None else jnp.logical_and(on, inside)
        return on

    for field, chans, ny, nz in ((g2, NA, HY, HZ), (g1, NB, FY, FZ)):
        high, wide = (nz + 1) * chans, (ny + 1) * L
        for row, col in (
            (slice(0, chans), slice(None)),
            (slice(high, high + chans), slice(None)),
            (slice(chans, high), slice(0, L)),
            (slice(chans, high), slice(wide, wide + L)),
        ):
            field[row, col] = jnp.zeros_like(field[row, col])
    rows1 = 3 * NC * FZ
    for field in (vh, vz, qy, qz):
        field[...] = jnp.zeros_like(field)
    s2[...] = jnp.zeros_like(s2)

    partners = [device(y=y, z=z) for y, z in around] + [device(d=1), device(d=-1)]
    along, across = rounds_of(sizes)
    rounds = [[device(d=d) for d in (2**step, -(2**step))] for step in range(along)]
    rounds += [[device(y=y, z=z) for y, z in around]]
    for step in range(1, across):
        far = []
        for axis, count in (("y", ngy), ("z", ngz)):
            if 2**step < count // 2:
                far += [device(**{axis: 2**step}), device(**{axis: -(2**step)})]
        rounds.append(far)

    def announce(step):
        for one in rounds[step]:
            pl.semaphore_signal(sem_r.at[step], inc=1, device_id=one, device_id_type=MESH)

    def hear(step):
        pl.semaphore_wait(sem_r.at[step], len(rounds[step]))
        if step + 1 not in (along, along + across):
            announce(step + 1)

    barrier = pltpu.get_barrier_semaphore()
    for one in partners:
        pl.semaphore_signal(barrier, inc=1, device_id=one, device_id_type=MESH)

    for load in loads[3:6]:
        load.wait()
    upf = upstream[...].astype(f32)
    e2 = (upf * slope_of(second[...].astype(f32))).astype(bf16).astype(f32)
    p2 = where_second[...].astype(f32)
    quarter = jnp.concatenate(
        [e2[:, z] for z in range(HZ // 2)] + [p2[:, z] for z in range(HZ // 2)], axis=0
    ).astype(bf16)
    by4 = one_hot(iota((L // 4, L), 1) // 4 == iota((L // 4, L), 0))
    quarter = dot(quarter, by4)
    half_x = ((iota((NA, L), 1) // 2) % 2).astype(f32)
    odd = iota((NA, L), 1) % 2 == 1
    tiles = {}
    for z in range(HZ // 2):
        e = quarter[z * NA : (z + 1) * NA]
        w = quarter[(HZ // 2 + z) * NA : (HZ // 2 + z + 1) * NA] - half_x
        for dy in range(2):
            for dz in range(2):
                tile = jnp.where(w == 4.0 * dy + 2.0 * dz, e, 0.0)
                row, col = (2 * z + dz + 1) * NA, (dy + 1) * L
                g2[row : row + NA, col : col + L] = tile.astype(bf16)
                tiles[2 * z + dz, dy] = tile
    for side, at_y, at_z in ((0, 0, 0), (1, HY - 1, HZ - 1)):
        for z in range(HZ // 2):
            pair = jnp.where(odd, tiles[2 * z + 1, at_y], tiles[2 * z, at_y])
            py[side, z * NA : (z + 1) * NA] = pair.astype(bf16)
        pz[side] = jnp.where(odd, tiles[at_z, 1], tiles[at_z, 0]).astype(bf16)

    def unpaired(value):
        value = value.astype(f32)
        even_half = jnp.where(odd, pltpu.roll(value, 1, 1), value)
        odd_half = jnp.where(odd, value, pltpu.roll(value, L - 1, 1))
        return even_half.astype(bf16), odd_half.astype(bf16)

    def put_volume(here, i, col):
        for tx, by in enumerate((1, 0, -1)):
            row = (tx * NC + i) * FZ
            v3[row : row + FZ, col : col + L] = (moved(here, by) if by else here).astype(bf16)

    loads[0].wait()
    for y in range(FY):
        value = vol[:, y].astype(f32)
        vf[0, y] = value[:, 0].astype(bf16)
        vf[1, y] = value[:, FZ - 1].astype(bf16)
        for i in range(NC):
            put_volume(value[i], i, (y + 1) * L)

    for load in loads[1:3] + loads[6:]:
        load.wait()
    by2 = one_hot(iota((L // 2, L), 1) // 2 == iota((L // 2, L), 0))
    halves = [first[:, y].astype(f32).reshape(NB * HZ, L // 2) for y in range(HY)]
    halves += [where_first[:, y].astype(f32).reshape(NB * HZ, L // 2) for y in range(HY)]
    halves = [dot(each.astype(bf16), by2).astype(bf16) for each in halves]
    r, c = iota((NB * HZ, NB * HZ), 0), iota((NB * HZ, NB * HZ), 1)
    order = one_hot(c == (r % NB) * HZ + r // NB)
    halves = dot(order, jnp.concatenate(halves, axis=1))
    pre1, p1 = halves[:, : HY * L], halves[:, HY * L :]
    slope1 = slope_of(pre1)
    act = jnp.where(pre1 > 0, pre1, LEAK * pre1).astype(bf16).astype(f32)

    pl.semaphore_wait(barrier, len(partners))

    def remote(src, dst, sems, index, to):
        return pltpu.make_async_remote_copy(
            src_ref=src,
            dst_ref=dst,
            send_sem=sems.at[0, index],
            recv_sem=sems.at[1, index],
            device_id=to,
            device_id_type=MESH,
        )

    def start(copies):
        for side, copy in copies:
            pl.when(exists(*side))(copy.start)

    def finish(copies):
        for (y, z), copy in copies:
            pl.when(exists(y, z))(copy.wait_send)
            pl.when(exists(-y, -z))(copy.wait_recv)

    def rim(field, chans, ny, nz, base):
        copies = []
        for index, (y, z) in enumerate(around):
            height, width = (1 if z else nz), (1 if y else ny)
            from_row, to_row = (nz if z > 0 else 1), {-1: nz + 1, 0: 1, 1: 0}[z]
            from_col, to_col = (ny if y > 0 else 1), {-1: ny + 1, 0: 1, 1: 0}[y]
            source = field.at[
                pl.ds(from_row * chans, height * chans), pl.ds(from_col * L, width * L)
            ]
            target = field.at[
                pl.ds(to_row * chans, height * chans), pl.ds(to_col * L, width * L)
            ]
            copies.append(
                ((y, z), remote(source, target, sem_h, base + index, device(y=y, z=z)))
            )
        return copies

    def volume_rim(base):
        copies = []
        for index, (y, z) in enumerate(around):
            if z == 0:
                source, target = vol.at[:, FY - 1 if y > 0 else 0], vh.at[0 if y > 0 else 1]
            else:
                from_y, to_y = (FY - 1 if y > 0 else 0), {-1: FY + 1, 0: 1, 1: 0}[y]
                width = 1 if y else FY
                source = vf.at[1 if z > 0 else 0, pl.ds(from_y, width)]
                target = vz.at[0 if z > 0 else 1, pl.ds(to_y, width)]
            copies.append(
                ((y, z), remote(source, target, sem_h, base + index, device(y=y, z=z)))
            )
        return copies

    def paired_rim(base):
        copies = []
        for index, (y, z) in enumerate(around):
            if y and z:
                row, to_row = (HZ if z > 0 else 1), (0 if z > 0 else HZ + 1)
                col, to_col = (HY if y > 0 else 1), (0 if y > 0 else HY + 1)
                source = g2.at[pl.ds(row * NA, NA), pl.ds(col * L, L)]
                target = g2.at[pl.ds(to_row * NA, NA), pl.ds(to_col * L, L)]
            else:
                up = 1 if y + z > 0 else 0
                source, target = (py.at[up], qy.at[1 - up]) if y else (pz.at[up], qz.at[1 - up])
            copies.append(
                ((y, z), remote(source, target, sem_h, base + index, device(y=y, z=z)))
            )
        return copies

    rim2, rim_v = paired_rim(0), volume_rim(8)
    start(rim2)
    start(rim_v)

    announce(0)
    announce(along)

    tiled = dot(k2[...], one_hot(iota((NA, (HZ + 2) * NA), 1) % NA == iota((NA, (HZ + 2) * NA), 0)))
    z_of = iota((NB, (HZ + 2) * NA), 1) // NA
    for ty in range(3):
        for tx in range(3):
            for z in range(HZ):
                block = jnp.zeros((NB, (HZ + 2) * NA), f32)
                for tz in range(3):
                    t = ((ty * 3 + tz) * 3 + tx) * NB
                    block = jnp.where(z_of == z - tz + 2, tiled[t : t + NB], block)
                row = ((ty * 3 + tx) * HZ + z) * NB
                w2[row : row + NB, :] = block.astype(bf16)

    hear(0)
    for y in range(HY):
        here = act[:, y * L : (y + 1) * L]
        for tx, by in enumerate((2, 0, -2)):
            value = (moved(here, by) if by else here).astype(bf16)
            for z in range(HZ):
                row = (z * 3 + tx) * NB
                a3[row : row + NB, y * L : (y + 1) * L] = value[z * NB : (z + 1) * NB]

    for step in range(1, along - 1):
        hear(step)
    hear(along)
    width = (FZ + 2) * NB
    tiled = dot(
        k1[...].astype(f32).reshape(27 * NC, NB).astype(bf16),
        one_hot(iota((NB, width), 1) % NB == iota((NB, width), 0)),
    )
    off = iota((FZ, width), 0) - iota((FZ, width), 1) // NB + 2
    for ty in range(3):
        for tx in range(3):
            for i in range(NC):
                block = jnp.zeros((FZ, width), f32)
                for tz in range(3):
                    t = ((ty * 3 + tz) * 3 + tx) * NC + i
                    line = jnp.broadcast_to(tiled[t : t + 1], (FZ, width))
                    block = jnp.where(off == tz, line, block)
                row = ((ty * 3 + tx) * NC + i) * FZ
                w1[row : row + FZ, :] = block.astype(bf16)

    finish(rim2)
    for side in range(2):
        row, col = side * (HZ + 1) * NA, side * (HY + 1) * L
        g2[row : row + NA, L : 2 * L], g2[row : row + NA, 2 * L : 3 * L] = unpaired(qz[side])
        for z in range(HZ // 2):
            low, high = unpaired(qy[side, z * NA : (z + 1) * NA])
            row = (2 * z + 1) * NA
            g2[row : row + NA, col : col + L] = low
            g2[row + NA : row + 2 * NA, col : col + L] = high

    for ty in range(3):
        taps = None
        for z in range(HZ):
            part = dot_t(
                g2[z * NA : (z + 3) * NA, (2 - ty) * L : (2 - ty + HY) * L],
                a3[z * 3 * NB : (z + 1) * 3 * NB, :],
            )
            taps = part if taps is None else taps + part
        taps = taps * (0.5 * scales[1])
        for tz in range(3):
            row = (ty * 3 + tz) * NA
            s2[row : row + NA, : 3 * NB] = taps[(2 - tz) * NA : (3 - tz) * NA]

    behind = per2 * 3 * NB
    def part_of_row(row, lane):
        value = s2[pl.ds(row, ndp, stride=per2), :]
        if msg2.shape[1] > L:
            rest = jnp.zeros((ndp, msg2.shape[1] - L), f32)
            value = jnp.concatenate([value, rest], axis=1)
        return pltpu.roll(value, lane, 1) if lane else value

    def masked(value, lane):
        at_lane = iota(value.shape, 1)
        return jnp.where(jnp.logical_and(at_lane >= lane, at_lane < lane + NB), value, 0.0)

    for tap in range(8):
        value = part_of_row(tap * NA, 0)
        for o in range(1, per2):
            value = value + part_of_row(tap * NA + o, o * 3 * NB)
        for piece in range(tap, 3 * per2, 8):
            lane, tx = behind + piece // 8 * NB, piece % 3
            moved_by = (lane - tx * NB) % msg2.shape[1]
            value = value + masked(part_of_row(8 * NA + piece // 3, moved_by), lane)
        msg2[pl.ds(tap, ndp, stride=8), :] = value

    def scatter(message, slots, base):
        copies = []
        for d in range(1, ndp):
            copy = remote(message(at(dp, d, ndp)), slots.at[d], sem_z, base + d, device(d=d))
            copy.start()
            copies.append(copy)
        return copies

    if along > 1:
        hear(along - 1)
    scatter2 = scatter(lambda k: msg2.at[pl.ds(pl.multiple_of(k * 8, 8), 8), :], rz2, 0)

    rows2 = 3 * HZ * NB
    total = None
    for ty in range(3):
        part = dot(w2[ty * rows2 : (ty + 1) * rows2, :], g2[:, (2 - ty) * L : (2 - ty + HY) * L])
        total = part if total is None else total + part
    third = HZ * NB
    low = spread_across_x(total[:third], -2)
    high = spread_across_x(total[2 * third :], 2)
    odd_x = (iota((NB, L), 1) % 2).astype(f32)
    for y in range(HY):
        e = total[third : 2 * third, y * L : (y + 1) * L] + low[y] + high[y]
        e = e * slope1[:, y * L : (y + 1) * L]
        w = p1[:, y * L : (y + 1) * L]
        for z in range(HZ):
            ez = e[z * NB : (z + 1) * NB]
            wz = w[z * NB : (z + 1) * NB] - odd_x
            for dy in range(2):
                for dz in range(2):
                    row, col = (2 * z + dz + 1) * NB, (2 * y + dy + 1) * L
                    tile = jnp.where(wz == 4.0 * dy + 2.0 * dz, ez, 0.0).astype(bf16)
                    g1[row : row + NB, col : col + L] = tile

    rim1 = rim(g1, NB, FY, FZ, 16)
    start(rim1)

    finish(rim_v)
    for side in range(2):
        for i in range(NC):
            put_volume(vh[side, i].astype(f32), i, side * (FY + 1) * L)
        for y in range(FY + 2):
            here = vz[side, y].astype(f32)
            layers = [moved(here, 1), here, moved(here, -1), jnp.zeros_like(here)]
            row = rows1 + side * NB
            v3[row : row + NB, y * L : (y + 1) * L] = jnp.concatenate(layers, axis=0).astype(bf16)

    count = rows1 + 2 * NB
    c = iota((NB, count), 1)
    z_of = jnp.where(c < rows1, c % FZ, jnp.where(c < rows1 + NB, -1, FZ))
    r, c = iota((count, L), 0), iota((count, L), 1)
    q = jnp.where(r < rows1, r // FZ, (r - rows1) % NB)
    lanes = one_hot(jnp.logical_and(q < 3 * NC, c == (q % NC) * 27 + q // NC))
    line = None
    for ty in range(3):
        part = dot_t(g1[NB : (FZ + 1) * NB, L : (FY + 1) * L], v3[:, ty * L : (ty + FY) * L])
        taps = []
        for tz in range(3):
            tap = None
            for z in range(FZ):
                add = jnp.where(z_of == z + tz - 1, part[z * NB : (z + 1) * NB], 0.0)
                tap = add if tap is None else tap + add
            taps.append(tap)
        taps = exactly(jnp.concatenate(taps, axis=0) * scales[0], lanes)
        for tz in range(3):
            tap = taps[tz * NB : (tz + 1) * NB]
            shift = (ty * 3 + tz) * 3
            tap = pltpu.roll(tap, shift, 1) if shift else tap
            line = tap if line is None else line + tap
    for k in range(ndp):
        for o in range(per1):
            row = k * per1 + o
            msg1[k, :, o * L : (o + 1) * L] = line[row : row + 1]

    scatter1 = scatter(lambda k: msg1.at[k], rz1, ndp)

    finish(rim1)

    total = None
    for ty in range(3):
        part = dot(w1[ty * rows1 : (ty + 1) * rows1, :], g1[:, (2 - ty) * L : (2 - ty + FY) * L])
        total = part if total is None else total + part
    third = NC * FZ
    low = spread_across_x(total[:third], -1)
    high = spread_across_x(total[2 * third :], 1)
    for y in range(FY):
        value = total[third : 2 * third, y * L : (y + 1) * L] + low[y] + high[y]
        for i in range(NC):
            grad_vol[i, y] = value[i * FZ : (i + 1) * FZ].astype(bf16)

    wide2 = pl.cdiv(out2.shape[0], L) * L
    r, c = iota((msg2.shape[1], wide2), 0), iota((msg2.shape[1], wide2), 1)
    of_row = (r // (3 * NB) * NB + r % NB) * 27 + r % (3 * NB) // NB
    to_main = one_hot(jnp.logical_and(r < behind, c == of_row))
    to_last = [
        one_hot(jnp.logical_and((r - behind) // NB == group, c == r % NB * 27))
        for group in range(pl.cdiv(3 * per2, 8))
    ]

    here = gy * ngz + gz

    def share(value, slots, base):
        slots[here] = value
        copies = []
        for index, (y, z) in enumerate(plane):
            copy = remote(slots.at[here], slots.at[here], sem_p, base + index, device(y=y, z=z))
            copy.start()
            copies.append(copy)
        return copies

    def gather(copies, slots):
        for copy in copies:
            copy.wait()
        value = slots[0]
        for d in range(1, ngy * ngz):
            value = value + slots[d]
        return value

    def reduce(copies, own, slots):
        for d, copy in enumerate(copies):
            copy.wait()
            own = own + slots[d + 1]
        return own

    for step in range(1, across):
        hear(along + step)
    own = msg2[pl.ds(pl.multiple_of(dp * 8, 8), 8), :]
    share2 = share(reduce(scatter2, own, rz2), rp2, 0)
    share1 = share(reduce(scatter1, msg1[dp], rz1), rp1, len(plane))

    sums = gather(share2, rp2)
    main = exactly(sums, to_main)
    line = None
    for tap in range(8):
        row = main[tap : tap + 1]
        row = pltpu.roll(row, 3 * tap, 1) if tap else row
        line = row if line is None else line + row
    last = [exactly(sums, lanes) for lanes in to_last]
    for piece in range(3 * per2):
        row = last[piece // 8][piece % 8 : piece % 8 + 1]
        line = line + pltpu.roll(row, piece // 3 * NB * 27 + 24 + piece % 3, 1)
    out2[...] = line[0, : out2.shape[0]]
    line = gather(share1, rp1)
    for o in range(per1):
        out1[o * NC * 27 : (o + 1) * NC * 27] = line[0, o * L : o * L + NC * 27]


def rounds_of(sizes):
    return [max(1, (most // 2 - 1).bit_length()) for most in (sizes[0], max(sizes[1:]))]


def shards(sizes, scales, volume, first, where_first, second, where_second, upstream, k1, k2):
    ndp, ngy, ngz = sizes
    k1 = jnp.transpose(k1, (2, 3, 4, 1, 0)).reshape(27, NC, NB)
    k2 = jnp.transpose(k2, (2, 3, 4, 1, 0)).reshape(27 * NB, NA)
    per2, per1 = NA // ndp, NB // ndp
    wide1 = per1 * L
    wide2 = pl.cdiv(per2 * 3 * NB + pl.cdiv(3 * per2, 8) * NB, L) * L
    there = ngy * ngz
    vmem = pl.BlockSpec(memory_space=pltpu.VMEM)
    arguments = (
        volume[0],
        first[0],
        where_first[0],
        second[0, :, 0],
        where_second[0, :, 0],
        upstream[0, :, 0],
        k1,
        k2,
    )
    grad_vol, first_out, second_out = pl.pallas_call(
        functools.partial(kernel, sizes, scales),
        out_shape=(
            jax.ShapeDtypeStruct((NC, FY, FZ, L), bf16),
            jax.ShapeDtypeStruct((per1 * NC * 27,), f32),
            jax.ShapeDtypeStruct((per2 * NB * 27,), f32),
        ),
        in_specs=[pl.BlockSpec(memory_space=pltpu.HBM)] * 8,
        out_specs=(vmem,) * 3,
        scratch_shapes=[
            pltpu.VMEM(((HZ + 2) * NA, (HY + 2) * L), bf16),
            pltpu.VMEM(((FZ + 2) * NB, (FY + 2) * L), bf16),
            pltpu.VMEM((9 * HZ * NB, (HZ + 2) * NA), bf16),
            pltpu.VMEM((9 * NC * FZ, (FZ + 2) * NB), bf16),
            pltpu.VMEM((HZ * 3 * NB, HY * L), bf16),
            pltpu.VMEM((3 * NC * FZ + 2 * NB, (FY + 2) * L), bf16),
            pltpu.VMEM((2, FY, NC, L), bf16),
            pltpu.VMEM((2, NC, FZ, L), bf16),
            pltpu.VMEM((2, FY + 2, NC, L), bf16),
            pltpu.VMEM((2, HZ // 2 * NA, L), bf16),
            pltpu.VMEM((2, NA, L), bf16),
            pltpu.VMEM((2, HZ // 2 * NA, L), bf16),
            pltpu.VMEM((2, NA, L), bf16),
            pltpu.VMEM((9 * NA, L), f32),
            pltpu.VMEM((ndp, 1, wide1), f32),
            pltpu.VMEM((ndp * 8, wide2), f32),
            pltpu.VMEM((ndp, 1, wide1), f32),
            pltpu.VMEM((ndp, 8, wide2), f32),
            pltpu.VMEM((there, 1, wide1), f32),
            pltpu.VMEM((there, 8, wide2), f32),
            pltpu.SemaphoreType.DMA((2, 24)),
            pltpu.SemaphoreType.DMA((2, 2 * ndp)),
            pltpu.SemaphoreType.DMA((2, 2 * there)),
            pltpu.SemaphoreType.REGULAR((sum(rounds_of(sizes)),)),
            *[pltpu.VMEM(one.shape, one.dtype) for one in arguments],
            pltpu.SemaphoreType.DMA((8,)),
        ],
        compiler_params=pltpu.CompilerParams(collective_id=0, has_side_effects=True),
    )(*arguments)
    return (grad_vol[None], first_out, second_out)


def solution(mesh):
    sizes = tuple(mesh.shape[axis] for axis in ("dp", "gy", "gz"))
    cells = sizes[0] * sizes[1] * sizes[2] * FY * FZ * L
    scales = (math.sqrt(8.0 / cells), math.sqrt(64.0 / cells))
    split = P("dp", None, "gy", "gz", None)
    return jax.shard_map(
        functools.partial(shards, sizes, scales),
        mesh=mesh,
        in_specs=(split,) * 6 + (P(), P()),
        out_specs=(split, P("dp"), P("dp")),
        check_vma=False,
    )
```

```python
import functools
import math

import jax
import jax.numpy as jnp
from jax import lax
from jax.experimental import pallas as pl
from jax.experimental.pallas import tpu as pltpu
from jax.sharding import PartitionSpec as P

MESH = pl.DeviceIdType.MESH
f32, bf16, i32 = jnp.float32, jnp.bfloat16, jnp.int32
LEAK = 0.3
L = 128
NA, NB, NC = 32, 16, 4
HY, HZ = 2, 8
FY, FZ = 4, 16


def iota(shape, dim):
    return lax.broadcasted_iota(i32, shape, dim)


def dot(a, b):
    return lax.dot_general(a, b, (((1,), (0,)), ((), ())), preferred_element_type=f32)


def dot_t(a, b, precision=None):
    return lax.dot_general(
        a, b, (((1,), (1,)), ((), ())), preferred_element_type=f32, precision=precision
    )


def one_hot(mask):
    return jnp.where(mask, 1.0, 0.0).astype(bf16)


def slope_of(pre):
    return jnp.where(pre > 0, 1.0, LEAK).astype(f32)


def moved(value, by):
    lane = iota(value.shape, 1)
    inside = lane >= by if by > 0 else lane < L + by
    return jnp.where(inside, pltpu.roll(value, by % L, 1), 0.0)


def spread_across_x(value, by):
    return [moved(value[:, at : at + L], by) for at in range(0, value.shape[1], L)]


def exactly(value, mask):
    high = value.astype(bf16).astype(f32)
    middle = (value - high).astype(bf16).astype(f32)
    pieces = jnp.concatenate([high, middle, value - high - middle], axis=0).astype(bf16)
    pieces = dot(pieces, mask)
    rows = value.shape[0]
    return pieces[:rows] + pieces[rows : 2 * rows] + pieces[2 * rows :]


def kernel(
    sizes,
    scales,
    *refs,
):
    arguments, refs = refs[:8], refs[8:]
    copied, refs = refs[-9:-1], refs[:-9] + refs[-1:]
    loads = [
        pltpu.make_async_copy(source, target, refs[-1].at[index])
        for index, (source, target) in enumerate(zip(arguments, copied))
    ]
    for load in loads:
        load.start()
    body(sizes, scales, loads, *copied, *refs[:-1])


def body(
    sizes,
    scales,
    loads,
    vol,
    first,
    where_first,
    second,
    where_second,
    upstream,
    k1,
    k2,
    grad_vol,
    out1,
    out2,
    g2,
    g1,
    w2,
    w1,
    a3,
    v3,
    vf,
    vh,
    vz,
    py,
    pz,
    qy,
    qz,
    s2,
    msg1,
    msg2,
    rz1,
    rz2,
    rp1,
    rp2,
    sem_h,
    sem_z,
    sem_p,
    sem_r,
):
    ndp, ngy, ngz = sizes
    per2, per1 = NA // ndp, NB // ndp
    dp, gy, gz = lax.axis_index("dp"), lax.axis_index("gy"), lax.axis_index("gz")

    def at(index, step, count):
        return lax.rem(index + (step + count), count)

    def device(d=0, y=0, z=0):
        return {"dp": at(dp, d, ndp), "gy": at(gy, y, ngy), "gz": at(gz, z, ngz)}

    around = [(y, z) for y in (-1, 0, 1) for z in (-1, 0, 1) if (y, z) != (0, 0)]
    plane = [(y, z) for y in range(ngy) for z in range(ngz) if (y, z) != (0, 0)]

    def hops(y, z):
        return min(z, ngz - z) * 2 + min(y, ngy - y)

    plane = sorted(plane, key=lambda one: -hops(*one))
    distances = sorted(range(1, ndp), key=lambda d: -min(d, ndp - d))

    def exists(y, z):
        on = None
        for step, index, count in ((y, gy, ngy), (z, gz, ngz)):
            if step:
                inside = index > 0 if step < 0 else index < count - 1
                on = inside if on is None else jnp.logical_and(on, inside)
        return on

    for field, chans, ny, nz in ((g2, NA, HY, HZ), (g1, NB, FY, FZ)):
        high, wide = (nz + 1) * chans, (ny + 1) * L
        for row, col in (
            (slice(0, chans), slice(None)),
            (slice(high, high + chans), slice(None)),
            (slice(chans, high), slice(0, L)),
            (slice(chans, high), slice(wide, wide + L)),
        ):
            field[row, col] = jnp.zeros_like(field[row, col])
    rows1 = 3 * NC * FZ
    for field in (vh, vz, qy, qz):
        field[...] = jnp.zeros_like(field)
    s2[...] = jnp.zeros_like(s2)

    near = reach(ndp)
    close = [(y % ngy, z % ngz) for y, z in around]
    partners = [device(y=y, z=z) for y, z in sorted(plane, key=lambda one: one not in close)]
    partners += [device(d=sign * d) for d in range(near, 0, -1) for sign in (1, -1)]
    rim_dp = [device(d=near), device(d=-near)] if near < ndp // 2 else []

    barrier = pltpu.get_barrier_semaphore()
    for one in partners:
        pl.semaphore_signal(barrier, inc=1, device_id=one, device_id_type=MESH)

    for load in loads[3:6]:
        load.wait()
    upf = upstream[...].astype(f32)
    e2 = (upf * slope_of(second[...].astype(f32))).astype(bf16).astype(f32)
    p2 = where_second[...].astype(f32)
    quarter = jnp.concatenate(
        [e2[:, z] for z in range(HZ // 2)] + [p2[:, z] for z in range(HZ // 2)], axis=0
    ).astype(bf16)
    by4 = one_hot(iota((L // 4, L), 1) // 4 == iota((L // 4, L), 0))
    quarter = dot(quarter, by4)
    half_x = ((iota((NA, L), 1) // 2) % 2).astype(f32)
    odd = iota((NA, L), 1) % 2 == 1
    tiles = {}
    for z in range(HZ // 2):
        e = quarter[z * NA : (z + 1) * NA]
        w = quarter[(HZ // 2 + z) * NA : (HZ // 2 + z + 1) * NA] - half_x
        for dy in range(2):
            for dz in range(2):
                tile = jnp.where(w == 4.0 * dy + 2.0 * dz, e, 0.0)
                row, col = (2 * z + dz + 1) * NA, (dy + 1) * L
                g2[row : row + NA, col : col + L] = tile.astype(bf16)
                tiles[2 * z + dz, dy] = tile
    for side, at_y, at_z in ((0, 0, 0), (1, HY - 1, HZ - 1)):
        for z in range(HZ // 2):
            pair = jnp.where(odd, tiles[2 * z + 1, at_y], tiles[2 * z, at_y])
            py[side, z * NA : (z + 1) * NA] = pair.astype(bf16)
        pz[side] = jnp.where(odd, tiles[at_z, 1], tiles[at_z, 0]).astype(bf16)

    def unpaired(value):
        value = value.astype(f32)
        even_half = jnp.where(odd, pltpu.roll(value, 1, 1), value)
        odd_half = jnp.where(odd, value, pltpu.roll(value, L - 1, 1))
        return even_half.astype(bf16), odd_half.astype(bf16)

    pl.semaphore_wait(barrier, len(partners))

    def remote(src, dst, sems, index, to):
        return pltpu.make_async_remote_copy(
            src_ref=src,
            dst_ref=dst,
            send_sem=sems.at[0, index],
            recv_sem=sems.at[1, index],
            device_id=to,
            device_id_type=MESH,
        )

    def start(copies):
        for side, copy in copies:
            pl.when(exists(*side))(copy.start)

    def finish(copies):
        for (y, z), copy in copies:
            pl.when(exists(y, z))(copy.wait_send)
            pl.when(exists(-y, -z))(copy.wait_recv)

    def rim(field, chans, ny, nz, base):
        copies = []
        for index, (y, z) in enumerate(around):
            height, width = (1 if z else nz), (1 if y else ny)
            from_row, to_row = (nz if z > 0 else 1), {-1: nz + 1, 0: 1, 1: 0}[z]
            from_col, to_col = (ny if y > 0 else 1), {-1: ny + 1, 0: 1, 1: 0}[y]
            source = field.at[
                pl.ds(from_row * chans, height * chans), pl.ds(from_col * L, width * L)
            ]
            target = field.at[
                pl.ds(to_row * chans, height * chans), pl.ds(to_col * L, width * L)
            ]
            copies.append(
                ((y, z), remote(source, target, sem_h, base + index, device(y=y, z=z)))
            )
        return copies

    def volume_rim(base):
        copies = []
        for index, (y, z) in enumerate(around):
            if z == 0:
                source, target = vol.at[:, FY - 1 if y > 0 else 0], vh.at[0 if y > 0 else 1]
            else:
                from_y, to_y = (FY - 1 if y > 0 else 0), {-1: FY + 1, 0: 1, 1: 0}[y]
                width = 1 if y else FY
                source = vf.at[1 if z > 0 else 0, pl.ds(from_y, width)]
                target = vz.at[0 if z > 0 else 1, pl.ds(to_y, width)]
            copies.append(
                ((y, z), remote(source, target, sem_h, base + index, device(y=y, z=z)))
            )
        return copies

    def paired_rim(base):
        copies = []
        for index, (y, z) in enumerate(around):
            if y and z:
                row, to_row = (HZ if z > 0 else 1), (0 if z > 0 else HZ + 1)
                col, to_col = (HY if y > 0 else 1), (0 if y > 0 else HY + 1)
                source = g2.at[pl.ds(row * NA, NA), pl.ds(col * L, L)]
                target = g2.at[pl.ds(to_row * NA, NA), pl.ds(to_col * L, L)]
            else:
                up = 1 if y + z > 0 else 0
                source, target = (py.at[up], qy.at[1 - up]) if y else (pz.at[up], qz.at[1 - up])
            copies.append(
                ((y, z), remote(source, target, sem_h, base + index, device(y=y, z=z)))
            )
        return copies

    rim2, rim_v = paired_rim(0), volume_rim(8)
    start(rim2)
    for one in rim_dp:
        pl.semaphore_signal(sem_r.at[0], inc=1, device_id=one, device_id_type=MESH)
    loads[0].wait()
    for y in range(FY):
        value = vol[:, y].astype(f32)
        vf[0, y] = value[:, 0].astype(bf16)
        vf[1, y] = value[:, FZ - 1].astype(bf16)
    start(rim_v)

    def put_volume(here, i, col):
        for tx, by in enumerate((1, 0, -1)):
            row = (tx * NC + i) * FZ
            v3[row : row + FZ, col : col + L] = (moved(here, by) if by else here).astype(bf16)

    for y in range(FY):
        for i in range(NC):
            put_volume(vol[i, y].astype(f32), i, (y + 1) * L)

    for load in loads[1:3] + loads[6:]:
        load.wait()
    by2 = one_hot(iota((L // 2, L), 1) // 2 == iota((L // 2, L), 0))
    halves = [first[:, y].astype(f32).reshape(NB * HZ, L // 2) for y in range(HY)]
    halves += [where_first[:, y].astype(f32).reshape(NB * HZ, L // 2) for y in range(HY)]
    halves = [dot(each.astype(bf16), by2).astype(bf16) for each in halves]
    r, c = iota((NB * HZ, NB * HZ), 0), iota((NB * HZ, NB * HZ), 1)
    order = one_hot(c == (r % NB) * HZ + r // NB)
    halves = dot(order, jnp.concatenate(halves, axis=1))
    pre1, p1 = halves[:, : HY * L], halves[:, HY * L :]
    slope1 = slope_of(pre1)
    act = jnp.where(pre1 > 0, pre1, LEAK * pre1).astype(bf16).astype(f32)

    tiled = dot(k2[...], one_hot(iota((NA, (HZ + 2) * NA), 1) % NA == iota((NA, (HZ + 2) * NA), 0)))
    z_of = iota((NB, (HZ + 2) * NA), 1) // NA
    for ty in range(3):
        for tx in range(3):
            for z in range(HZ):
                block = jnp.zeros((NB, (HZ + 2) * NA), f32)
                for tz in range(3):
                    t = ((ty * 3 + tz) * 3 + tx) * NB
                    block = jnp.where(z_of == z - tz + 2, tiled[t : t + NB], block)
                row = ((ty * 3 + tx) * HZ + z) * NB
                w2[row : row + NB, :] = block.astype(bf16)

    for y in range(HY):
        here = act[:, y * L : (y + 1) * L]
        for tx, by in enumerate((2, 0, -2)):
            value = (moved(here, by) if by else here).astype(bf16)
            for z in range(HZ):
                row = (z * 3 + tx) * NB
                a3[row : row + NB, y * L : (y + 1) * L] = value[z * NB : (z + 1) * NB]

    width = (FZ + 2) * NB
    tiled = dot(
        k1[...].astype(f32).reshape(27 * NC, NB).astype(bf16),
        one_hot(iota((NB, width), 1) % NB == iota((NB, width), 0)),
    )
    off = iota((FZ, width), 0) - iota((FZ, width), 1) // NB + 2
    for ty in range(3):
        for tx in range(3):
            for i in range(NC):
                block = jnp.zeros((FZ, width), f32)
                for tz in range(3):
                    t = ((ty * 3 + tz) * 3 + tx) * NC + i
                    line = jnp.broadcast_to(tiled[t : t + 1], (FZ, width))
                    block = jnp.where(off == tz, line, block)
                row = ((ty * 3 + tx) * NC + i) * FZ
                w1[row : row + FZ, :] = block.astype(bf16)

    finish(rim2)
    for side in range(2):
        row, col = side * (HZ + 1) * NA, side * (HY + 1) * L
        g2[row : row + NA, L : 2 * L], g2[row : row + NA, 2 * L : 3 * L] = unpaired(qz[side])
        for z in range(HZ // 2):
            low, high = unpaired(qy[side, z * NA : (z + 1) * NA])
            row = (2 * z + 1) * NA
            g2[row : row + NA, col : col + L] = low
            g2[row + NA : row + 2 * NA, col : col + L] = high

    for ty in range(3):
        taps = None
        for z in range(HZ):
            part = dot_t(
                g2[z * NA : (z + 3) * NA, (2 - ty) * L : (2 - ty + HY) * L],
                a3[z * 3 * NB : (z + 1) * 3 * NB, :],
            )
            taps = part if taps is None else taps + part
        taps = taps * (0.5 * scales[1])
        for tz in range(3):
            row = (ty * 3 + tz) * NA
            s2[row : row + NA, : 3 * NB] = taps[(2 - tz) * NA : (3 - tz) * NA]

    behind = per2 * 3 * NB
    def part_of_row(row, lane):
        value = s2[pl.ds(row, ndp, stride=per2), :]
        if msg2.shape[1] > L:
            rest = jnp.zeros((ndp, msg2.shape[1] - L), f32)
            value = jnp.concatenate([value, rest], axis=1)
        return pltpu.roll(value, lane, 1) if lane else value

    def masked(value, lane):
        at_lane = iota(value.shape, 1)
        return jnp.where(jnp.logical_and(at_lane >= lane, at_lane < lane + NB), value, 0.0)

    for tap in range(8):
        value = part_of_row(tap * NA, 0)
        for o in range(1, per2):
            value = value + part_of_row(tap * NA + o, o * 3 * NB)
        for piece in range(tap, 3 * per2, 8):
            lane, tx = behind + piece // 8 * NB, piece % 3
            moved_by = (lane - tx * NB) % msg2.shape[1]
            value = value + masked(part_of_row(8 * NA + piece // 3, moved_by), lane)
        msg2[pl.ds(tap, ndp, stride=8), :] = value

    def scatter(message, slots, base):
        copies = []
        for d in distances:
            copy = remote(message(at(dp, d, ndp)), slots.at[d], sem_z, base + d, device(d=d))
            copy.start()
            copies.append(copy)
        return copies

    if rim_dp:
        pl.semaphore_wait(sem_r.at[0], len(rim_dp))
    scatter2 = scatter(lambda k: msg2.at[pl.ds(pl.multiple_of(k * 8, 8), 8), :], rz2, 0)

    rows2 = 3 * HZ * NB
    total = None
    for ty in range(3):
        part = dot(w2[ty * rows2 : (ty + 1) * rows2, :], g2[:, (2 - ty) * L : (2 - ty + HY) * L])
        total = part if total is None else total + part
    third = HZ * NB
    low = spread_across_x(total[:third], -2)
    high = spread_across_x(total[2 * third :], 2)
    odd_x = (iota((NB, L), 1) % 2).astype(f32)
    for y in range(HY):
        e = total[third : 2 * third, y * L : (y + 1) * L] + low[y] + high[y]
        e = e * slope1[:, y * L : (y + 1) * L]
        w = p1[:, y * L : (y + 1) * L]
        for z in range(HZ):
            ez = e[z * NB : (z + 1) * NB]
            wz = w[z * NB : (z + 1) * NB] - odd_x
            for dy in range(2):
                for dz in range(2):
                    row, col = (2 * z + dz + 1) * NB, (2 * y + dy + 1) * L
                    tile = jnp.where(wz == 4.0 * dy + 2.0 * dz, ez, 0.0).astype(bf16)
                    g1[row : row + NB, col : col + L] = tile

    rim1 = rim(g1, NB, FY, FZ, 16)
    start(rim1)

    finish(rim_v)
    for side in range(2):
        for i in range(NC):
            put_volume(vh[side, i].astype(f32), i, side * (FY + 1) * L)
        for y in range(FY + 2):
            here = vz[side, y].astype(f32)
            layers = [moved(here, 1), here, moved(here, -1), jnp.zeros_like(here)]
            row = rows1 + side * NB
            v3[row : row + NB, y * L : (y + 1) * L] = jnp.concatenate(layers, axis=0).astype(bf16)

    count = rows1 + 2 * NB
    c = iota((NB, count), 1)
    z_of = jnp.where(c < rows1, c % FZ, jnp.where(c < rows1 + NB, -1, FZ))
    r, c = iota((count, L), 0), iota((count, L), 1)
    q = jnp.where(r < rows1, r // FZ, (r - rows1) % NB)
    lanes = one_hot(jnp.logical_and(q < 3 * NC, c == (q % NC) * 27 + q // NC))
    line = None
    for ty in range(3):
        part = dot_t(g1[NB : (FZ + 1) * NB, L : (FY + 1) * L], v3[:, ty * L : (ty + FY) * L])
        taps = []
        for tz in range(3):
            tap = None
            for z in range(FZ):
                add = jnp.where(z_of == z + tz - 1, part[z * NB : (z + 1) * NB], 0.0)
                tap = add if tap is None else tap + add
            taps.append(tap)
        taps = exactly(jnp.concatenate(taps, axis=0) * scales[0], lanes)
        for tz in range(3):
            tap = taps[tz * NB : (tz + 1) * NB]
            shift = (ty * 3 + tz) * 3
            tap = pltpu.roll(tap, shift, 1) if shift else tap
            line = tap if line is None else line + tap
    for k in range(ndp):
        for o in range(per1):
            row = k * per1 + o
            msg1[k, :, o * L : (o + 1) * L] = line[row : row + 1]

    scatter1 = scatter(lambda k: msg1.at[k], rz1, ndp)

    finish(rim1)

    total = None
    for ty in range(3):
        part = dot(w1[ty * rows1 : (ty + 1) * rows1, :], g1[:, (2 - ty) * L : (2 - ty + FY) * L])
        total = part if total is None else total + part
    third = NC * FZ
    low = spread_across_x(total[:third], -1)
    high = spread_across_x(total[2 * third :], 1)
    for y in range(FY):
        value = total[third : 2 * third, y * L : (y + 1) * L] + low[y] + high[y]
        for i in range(NC):
            grad_vol[i, y] = value[i * FZ : (i + 1) * FZ].astype(bf16)

    wide2 = pl.cdiv(out2.shape[0], L) * L
    r, c = iota((msg2.shape[1], wide2), 0), iota((msg2.shape[1], wide2), 1)
    of_row = (r // (3 * NB) * NB + r % NB) * 27 + r % (3 * NB) // NB
    to_main = one_hot(jnp.logical_and(r < behind, c == of_row))
    to_last = [
        one_hot(jnp.logical_and((r - behind) // NB == group, c == r % NB * 27))
        for group in range(pl.cdiv(3 * per2, 8))
    ]

    here = gy * ngz + gz

    def share(value, slots, base):
        slots[here] = value
        copies = []
        for index, (y, z) in enumerate(plane):
            copy = remote(slots.at[here], slots.at[here], sem_p, base + index, device(y=y, z=z))
            copy.start()
            copies.append(copy)
        return copies

    def gather(copies, slots):
        for copy in copies:
            copy.wait()
        value = slots[0]
        for d in range(1, ngy * ngz):
            value = value + slots[d]
        return value

    def reduce(copies, own, slots):
        for copy in copies:
            copy.wait()
        for d in range(1, ndp):
            own = own + slots[d]
        return own

    own = msg2[pl.ds(pl.multiple_of(dp * 8, 8), 8), :]
    share2 = share(reduce(scatter2, own, rz2), rp2, 0)
    share1 = share(reduce(scatter1, msg1[dp], rz1), rp1, len(plane))

    sums = gather(share2, rp2)
    main = exactly(sums, to_main)
    line = None
    for tap in range(8):
        row = main[tap : tap + 1]
        row = pltpu.roll(row, 3 * tap, 1) if tap else row
        line = row if line is None else line + row
    last = [exactly(sums, lanes) for lanes in to_last]
    for piece in range(3 * per2):
        row = last[piece // 8][piece % 8 : piece % 8 + 1]
        line = line + pltpu.roll(row, piece // 3 * NB * 27 + 24 + piece % 3, 1)
    out2[...] = line[0, : out2.shape[0]]
    line = gather(share1, rp1)
    for o in range(per1):
        out1[o * NC * 27 : (o + 1) * NC * 27] = line[0, o * L : o * L + NC * 27]


def reach(ndp):
    return max(1, ndp // 4)


def handed_on(*refs):
    for source, target in zip(refs[:3], refs[3:]):
        target[...] = source[...]


def shards(sizes, scales, volume, first, where_first, second, where_second, upstream, k1, k2):
    ndp, ngy, ngz = sizes
    k1 = jnp.transpose(k1, (2, 3, 4, 1, 0)).reshape(27, NC, NB)
    k2 = jnp.transpose(k2, (2, 3, 4, 1, 0)).reshape(27 * NB, NA)
    per2, per1 = NA // ndp, NB // ndp
    wide1 = per1 * L
    wide2 = pl.cdiv(per2 * 3 * NB + pl.cdiv(3 * per2, 8) * NB, L) * L
    there = ngy * ngz
    vmem = pl.BlockSpec(memory_space=pltpu.VMEM)
    arguments = (
        volume[0],
        first[0],
        where_first[0],
        second[0, :, 0],
        where_second[0, :, 0],
        upstream[0, :, 0],
        k1,
        k2,
    )
    results = pl.pallas_call(
        functools.partial(kernel, sizes, scales),
        out_shape=(
            jax.ShapeDtypeStruct((NC, FY, FZ, L), bf16),
            jax.ShapeDtypeStruct((per1 * NC * 27,), f32),
            jax.ShapeDtypeStruct((per2 * NB * 27,), f32),
        ),
        in_specs=[pl.BlockSpec(memory_space=pltpu.HBM)] * 8,
        out_specs=(vmem,) * 3,
        scratch_shapes=[
            pltpu.VMEM(((HZ + 2) * NA, (HY + 2) * L), bf16),
            pltpu.VMEM(((FZ + 2) * NB, (FY + 2) * L), bf16),
            pltpu.VMEM((9 * HZ * NB, (HZ + 2) * NA), bf16),
            pltpu.VMEM((9 * NC * FZ, (FZ + 2) * NB), bf16),
            pltpu.VMEM((HZ * 3 * NB, HY * L), bf16),
            pltpu.VMEM((3 * NC * FZ + 2 * NB, (FY + 2) * L), bf16),
            pltpu.VMEM((2, FY, NC, L), bf16),
            pltpu.VMEM((2, NC, FZ, L), bf16),
            pltpu.VMEM((2, FY + 2, NC, L), bf16),
            pltpu.VMEM((2, HZ // 2 * NA, L), bf16),
            pltpu.VMEM((2, NA, L), bf16),
            pltpu.VMEM((2, HZ // 2 * NA, L), bf16),
            pltpu.VMEM((2, NA, L), bf16),
            pltpu.VMEM((9 * NA, L), f32),
            pltpu.VMEM((ndp, 1, wide1), f32),
            pltpu.VMEM((ndp * 8, wide2), f32),
            pltpu.VMEM((ndp, 1, wide1), f32),
            pltpu.VMEM((ndp, 8, wide2), f32),
            pltpu.VMEM((there, 1, wide1), f32),
            pltpu.VMEM((there, 8, wide2), f32),
            pltpu.SemaphoreType.DMA((2, 24)),
            pltpu.SemaphoreType.DMA((2, 2 * ndp)),
            pltpu.SemaphoreType.DMA((2, 2 * there)),
            pltpu.SemaphoreType.REGULAR((1,)),
            *[pltpu.VMEM(one.shape, one.dtype) for one in arguments],
            pltpu.SemaphoreType.DMA((8,)),
        ],
        compiler_params=pltpu.CompilerParams(collective_id=0, has_side_effects=True),
    )(*arguments)
    grad_vol, first_out, second_out = pl.pallas_call(
        handed_on,
        out_shape=tuple(jax.ShapeDtypeStruct(one.shape, one.dtype) for one in results),
        in_specs=[vmem] * 3,
        out_specs=(vmem,) * 3,

    )(*results)
    return (grad_vol[None], first_out, second_out)


def solution(mesh):
    sizes = tuple(mesh.shape[axis] for axis in ("dp", "gy", "gz"))
    cells = sizes[0] * sizes[1] * sizes[2] * FY * FZ * L
    scales = (math.sqrt(8.0 / cells), math.sqrt(64.0 / cells))
    split = P("dp", None, "gy", "gz", None)
    return jax.shard_map(
        functools.partial(shards, sizes, scales),
        mesh=mesh,
        in_specs=(split,) * 6 + (P(), P()),
        out_specs=(split, P("dp"), P("dp")),
        check_vma=False,
    )
```

```python
import functools
import math

import jax
import jax.numpy as jnp
from jax import lax
from jax.experimental import pallas as pl
from jax.experimental.pallas import tpu as pltpu
from jax.sharding import PartitionSpec as P

MESH = pl.DeviceIdType.MESH
f32, bf16, i32 = jnp.float32, jnp.bfloat16, jnp.int32
LEAK = 0.3
L = 128
NA, NB, NC = 32, 16, 4
HY, HZ = 2, 8
FY, FZ = 4, 16


def iota(shape, dim):
    return lax.broadcasted_iota(i32, shape, dim)


def dot(a, b):
    return lax.dot_general(a, b, (((1,), (0,)), ((), ())), preferred_element_type=f32)


def dot_t(a, b, precision=None):
    return lax.dot_general(
        a, b, (((1,), (1,)), ((), ())), preferred_element_type=f32, precision=precision
    )


def one_hot(mask):
    return jnp.where(mask, 1.0, 0.0).astype(bf16)


def slope_of(pre):
    return jnp.where(pre > 0, 1.0, LEAK).astype(f32)


def moved(value, by):
    lane = iota(value.shape, 1)
    inside = lane >= by if by > 0 else lane < L + by
    return jnp.where(inside, pltpu.roll(value, by % L, 1), 0.0)


def spread_across_x(value, by):
    return [moved(value[:, at : at + L], by) for at in range(0, value.shape[1], L)]


def exactly(value, mask):
    high = value.astype(bf16).astype(f32)
    middle = (value - high).astype(bf16).astype(f32)
    pieces = jnp.concatenate([high, middle, value - high - middle], axis=0).astype(bf16)
    pieces = dot(pieces, mask)
    rows = value.shape[0]
    return pieces[:rows] + pieces[rows : 2 * rows] + pieces[2 * rows :]


def kernel(
    sizes,
    scales,
    *refs,
):
    arguments, refs = refs[:8], refs[8:]
    copied, refs = refs[-9:-1], refs[:-9] + refs[-1:]
    loads = [
        pltpu.make_async_copy(source, target, refs[-1].at[index])
        for index, (source, target) in enumerate(zip(arguments, copied))
    ]
    for load in loads[3:6] + loads[:3] + loads[6:]:
        load.start()
    body(sizes, scales, loads, *copied, *refs[:-1])


def body(
    sizes,
    scales,
    loads,
    vol,
    first,
    where_first,
    second,
    where_second,
    upstream,
    k1,
    k2,
    grad_vol,
    out1,
    out2,
    g2,
    g1,
    w2,
    w1,
    a3,
    v3,
    vf,
    vh,
    vz,
    py,
    pz,
    qy,
    qz,
    s2,
    msg1,
    msg2,
    rz1,
    rz2,
    rp1,
    rp2,
    sem_h,
    sem_z,
    sem_p,
    sem_r,
):
    ndp, ngy, ngz = sizes
    per2, per1 = NA // ndp, NB // ndp
    dp, gy, gz = lax.axis_index("dp"), lax.axis_index("gy"), lax.axis_index("gz")

    def at(index, step, count):
        return lax.rem(index + (step + count), count)

    def device(d=0, y=0, z=0):
        return {"dp": at(dp, d, ndp), "gy": at(gy, y, ngy), "gz": at(gz, z, ngz)}

    around = [(y, z) for y in (-1, 0, 1) for z in (-1, 0, 1) if (y, z) != (0, 0)]
    plane = [(y, z) for y in range(ngy) for z in range(ngz) if (y, z) != (0, 0)]

    def hops(y, z):
        return min(z, ngz - z) * 2 + min(y, ngy - y)

    plane = sorted(plane, key=lambda one: -hops(*one))
    distances = sorted(range(1, ndp), key=lambda d: -min(d, ndp - d))

    def exists(y, z):
        on = None
        for step, index, count in ((y, gy, ngy), (z, gz, ngz)):
            if step:
                inside = index > 0 if step < 0 else index < count - 1
                on = inside if on is None else jnp.logical_and(on, inside)
        return on

    for field, chans, ny, nz in ((g2, NA, HY, HZ), (g1, NB, FY, FZ)):
        high, wide = (nz + 1) * chans, (ny + 1) * L
        for row, col in (
            (slice(0, chans), slice(None)),
            (slice(high, high + chans), slice(None)),
            (slice(chans, high), slice(0, L)),
            (slice(chans, high), slice(wide, wide + L)),
        ):
            field[row, col] = jnp.zeros_like(field[row, col])
    rows1 = 3 * NC * FZ
    for field in (vh, vz, qy, qz):
        field[...] = jnp.zeros_like(field)
    s2[...] = jnp.zeros_like(s2)

    near = reach(ndp)
    partners = [device(y=y, z=z) for y, z in around]
    far = [device(z=2), device(z=-2)] if 2 < ngz // 2 else []

    def tell(step, those):
        for one in those:
            pl.semaphore_signal(sem_r.at[step], inc=1, device_id=one, device_id_type=MESH)

    partners += [device(d=sign * d) for d in range(near, 0, -1) for sign in (1, -1)]
    rim_dp = [device(d=near), device(d=-near)] if near < ndp // 2 else []

    barrier = pltpu.get_barrier_semaphore()
    for one in partners:
        pl.semaphore_signal(barrier, inc=1, device_id=one, device_id_type=MESH)

    for load in loads[3:6]:
        load.wait()
    upf = upstream[...].astype(f32)
    e2 = (upf * slope_of(second[...].astype(f32))).astype(bf16).astype(f32)
    p2 = where_second[...].astype(f32)
    quarter = jnp.concatenate(
        [e2[:, z] for z in range(HZ // 2)] + [p2[:, z] for z in range(HZ // 2)], axis=0
    ).astype(bf16)
    by4 = one_hot(iota((L // 4, L), 1) // 4 == iota((L // 4, L), 0))
    quarter = dot(quarter, by4)
    half_x = ((iota((NA, L), 1) // 2) % 2).astype(f32)
    odd = iota((NA, L), 1) % 2 == 1
    tiles = {}
    for z in range(HZ // 2):
        e = quarter[z * NA : (z + 1) * NA]
        w = quarter[(HZ // 2 + z) * NA : (HZ // 2 + z + 1) * NA] - half_x
        for dy in range(2):
            for dz in range(2):
                tile = jnp.where(w == 4.0 * dy + 2.0 * dz, e, 0.0)
                row, col = (2 * z + dz + 1) * NA, (dy + 1) * L
                g2[row : row + NA, col : col + L] = tile.astype(bf16)
                tiles[2 * z + dz, dy] = tile
    for side, at_y, at_z in ((0, 0, 0), (1, HY - 1, HZ - 1)):
        for z in range(HZ // 2):
            pair = jnp.where(odd, tiles[2 * z + 1, at_y], tiles[2 * z, at_y])
            py[side, z * NA : (z + 1) * NA] = pair.astype(bf16)
        pz[side] = jnp.where(odd, tiles[at_z, 1], tiles[at_z, 0]).astype(bf16)

    def unpaired(value):
        value = value.astype(f32)
        even_half = jnp.where(odd, pltpu.roll(value, 1, 1), value)
        odd_half = jnp.where(odd, value, pltpu.roll(value, L - 1, 1))
        return even_half.astype(bf16), odd_half.astype(bf16)

    pl.semaphore_wait(barrier, len(partners))

    def remote(src, dst, sems, index, to):
        return pltpu.make_async_remote_copy(
            src_ref=src,
            dst_ref=dst,
            send_sem=sems.at[0, index],
            recv_sem=sems.at[1, index],
            device_id=to,
            device_id_type=MESH,
        )

    def start(copies):
        for side, copy in copies:
            pl.when(exists(*side))(copy.start)

    def finish(copies):
        for (y, z), copy in copies:
            pl.when(exists(y, z))(copy.wait_send)
            pl.when(exists(-y, -z))(copy.wait_recv)

    def rim(field, chans, ny, nz, base):
        copies = []
        for index, (y, z) in enumerate(around):
            height, width = (1 if z else nz), (1 if y else ny)
            from_row, to_row = (nz if z > 0 else 1), {-1: nz + 1, 0: 1, 1: 0}[z]
            from_col, to_col = (ny if y > 0 else 1), {-1: ny + 1, 0: 1, 1: 0}[y]
            source = field.at[
                pl.ds(from_row * chans, height * chans), pl.ds(from_col * L, width * L)
            ]
            target = field.at[
                pl.ds(to_row * chans, height * chans), pl.ds(to_col * L, width * L)
            ]
            copies.append(
                ((y, z), remote(source, target, sem_h, base + index, device(y=y, z=z)))
            )
        return copies

    def volume_rim(base):
        copies = []
        for index, (y, z) in enumerate(around):
            if z == 0:
                source, target = vol.at[:, FY - 1 if y > 0 else 0], vh.at[0 if y > 0 else 1]
            else:
                from_y, to_y = (FY - 1 if y > 0 else 0), {-1: FY + 1, 0: 1, 1: 0}[y]
                width = 1 if y else FY
                source = vf.at[1 if z > 0 else 0, pl.ds(from_y, width)]
                target = vz.at[0 if z > 0 else 1, pl.ds(to_y, width)]
            copies.append(
                ((y, z), remote(source, target, sem_h, base + index, device(y=y, z=z)))
            )
        return copies

    def paired_rim(base):
        copies = []
        for index, (y, z) in enumerate(around):
            if y and z:
                row, to_row = (HZ if z > 0 else 1), (0 if z > 0 else HZ + 1)
                col, to_col = (HY if y > 0 else 1), (0 if y > 0 else HY + 1)
                source = g2.at[pl.ds(row * NA, NA), pl.ds(col * L, L)]
                target = g2.at[pl.ds(to_row * NA, NA), pl.ds(to_col * L, L)]
            else:
                up = 1 if y + z > 0 else 0
                source, target = (py.at[up], qy.at[1 - up]) if y else (pz.at[up], qz.at[1 - up])
            copies.append(
                ((y, z), remote(source, target, sem_h, base + index, device(y=y, z=z)))
            )
        return copies

    rim2, rim_v = paired_rim(0), volume_rim(8)
    start(rim2)
    tell(0, rim_dp)
    tell(1, [device(y=y, z=z) for y, z in around])
    loads[0].wait()
    for y in range(FY):
        value = vol[:, y].astype(f32)
        vf[0, y] = value[:, 0].astype(bf16)
        vf[1, y] = value[:, FZ - 1].astype(bf16)
    start(rim_v)

    def put_volume(here, i, col):
        for tx, by in enumerate((1, 0, -1)):
            row = (tx * NC + i) * FZ
            v3[row : row + FZ, col : col + L] = (moved(here, by) if by else here).astype(bf16)

    for y in range(FY):
        for i in range(NC):
            put_volume(vol[i, y].astype(f32), i, (y + 1) * L)

    for load in loads[1:3] + loads[6:]:
        load.wait()
    by2 = one_hot(iota((L // 2, L), 1) // 2 == iota((L // 2, L), 0))
    halves = [first[:, y].astype(f32).reshape(NB * HZ, L // 2) for y in range(HY)]
    halves += [where_first[:, y].astype(f32).reshape(NB * HZ, L // 2) for y in range(HY)]
    halves = [dot(each.astype(bf16), by2).astype(bf16) for each in halves]
    r, c = iota((NB * HZ, NB * HZ), 0), iota((NB * HZ, NB * HZ), 1)
    order = one_hot(c == (r % NB) * HZ + r // NB)
    halves = dot(order, jnp.concatenate(halves, axis=1))
    pre1, p1 = halves[:, : HY * L], halves[:, HY * L :]
    slope1 = slope_of(pre1)
    act = jnp.where(pre1 > 0, pre1, LEAK * pre1).astype(bf16).astype(f32)

    tiled = dot(k2[...], one_hot(iota((NA, (HZ + 2) * NA), 1) % NA == iota((NA, (HZ + 2) * NA), 0)))
    z_of = iota((NB, (HZ + 2) * NA), 1) // NA
    for ty in range(3):
        for tx in range(3):
            for z in range(HZ):
                block = jnp.zeros((NB, (HZ + 2) * NA), f32)
                for tz in range(3):
                    t = ((ty * 3 + tz) * 3 + tx) * NB
                    block = jnp.where(z_of == z - tz + 2, tiled[t : t + NB], block)
                row = ((ty * 3 + tx) * HZ + z) * NB
                w2[row : row + NB, :] = block.astype(bf16)

    for y in range(HY):
        here = act[:, y * L : (y + 1) * L]
        for tx, by in enumerate((2, 0, -2)):
            value = (moved(here, by) if by else here).astype(bf16)
            for z in range(HZ):
                row = (z * 3 + tx) * NB
                a3[row : row + NB, y * L : (y + 1) * L] = value[z * NB : (z + 1) * NB]

    width = (FZ + 2) * NB
    tiled = dot(
        k1[...].astype(f32).reshape(27 * NC, NB).astype(bf16),
        one_hot(iota((NB, width), 1) % NB == iota((NB, width), 0)),
    )
    off = iota((FZ, width), 0) - iota((FZ, width), 1) // NB + 2
    for ty in range(3):
        for tx in range(3):
            for i in range(NC):
                block = jnp.zeros((FZ, width), f32)
                for tz in range(3):
                    t = ((ty * 3 + tz) * 3 + tx) * NC + i
                    line = jnp.broadcast_to(tiled[t : t + 1], (FZ, width))
                    block = jnp.where(off == tz, line, block)
                row = ((ty * 3 + tx) * NC + i) * FZ
                w1[row : row + FZ, :] = block.astype(bf16)

    finish(rim2)
    pl.semaphore_wait(sem_r.at[1], len(around))
    tell(2, far)
    for side in range(2):
        row, col = side * (HZ + 1) * NA, side * (HY + 1) * L
        g2[row : row + NA, L : 2 * L], g2[row : row + NA, 2 * L : 3 * L] = unpaired(qz[side])
        for z in range(HZ // 2):
            low, high = unpaired(qy[side, z * NA : (z + 1) * NA])
            row = (2 * z + 1) * NA
            g2[row : row + NA, col : col + L] = low
            g2[row + NA : row + 2 * NA, col : col + L] = high

    for ty in range(3):
        taps = None
        for z in range(HZ):
            part = dot_t(
                g2[z * NA : (z + 3) * NA, (2 - ty) * L : (2 - ty + HY) * L],
                a3[z * 3 * NB : (z + 1) * 3 * NB, :],
            )
            taps = part if taps is None else taps + part
        taps = taps * (0.5 * scales[1])
        for tz in range(3):
            row = (ty * 3 + tz) * NA
            s2[row : row + NA, : 3 * NB] = taps[(2 - tz) * NA : (3 - tz) * NA]

    behind = per2 * 3 * NB
    def part_of_row(row, lane):
        value = s2[pl.ds(row, ndp, stride=per2), :]
        if msg2.shape[1] > L:
            rest = jnp.zeros((ndp, msg2.shape[1] - L), f32)
            value = jnp.concatenate([value, rest], axis=1)
        return pltpu.roll(value, lane, 1) if lane else value

    def masked(value, lane):
        at_lane = iota(value.shape, 1)
        return jnp.where(jnp.logical_and(at_lane >= lane, at_lane < lane + NB), value, 0.0)

    for tap in range(8):
        value = part_of_row(tap * NA, 0)
        for o in range(1, per2):
            value = value + part_of_row(tap * NA + o, o * 3 * NB)
        for piece in range(tap, 3 * per2, 8):
            lane, tx = behind + piece // 8 * NB, piece % 3
            moved_by = (lane - tx * NB) % msg2.shape[1]
            value = value + masked(part_of_row(8 * NA + piece // 3, moved_by), lane)
        msg2[pl.ds(tap, ndp, stride=8), :] = value

    def scatter(message, slots, base):
        copies = []
        for d in distances:
            copy = remote(message(at(dp, d, ndp)), slots.at[d], sem_z, base + d, device(d=d))
            copy.start()
            copies.append(copy)
        return copies

    if rim_dp:
        pl.semaphore_wait(sem_r.at[0], len(rim_dp))
    scatter2 = scatter(lambda k: msg2.at[pl.ds(pl.multiple_of(k * 8, 8), 8), :], rz2, 0)

    rows2 = 3 * HZ * NB
    total = None
    for ty in range(3):
        part = dot(w2[ty * rows2 : (ty + 1) * rows2, :], g2[:, (2 - ty) * L : (2 - ty + HY) * L])
        total = part if total is None else total + part
    third = HZ * NB
    low = spread_across_x(total[:third], -2)
    high = spread_across_x(total[2 * third :], 2)
    odd_x = (iota((NB, L), 1) % 2).astype(f32)
    for y in range(HY):
        e = total[third : 2 * third, y * L : (y + 1) * L] + low[y] + high[y]
        e = e * slope1[:, y * L : (y + 1) * L]
        w = p1[:, y * L : (y + 1) * L]
        for z in range(HZ):
            ez = e[z * NB : (z + 1) * NB]
            wz = w[z * NB : (z + 1) * NB] - odd_x
            for dy in range(2):
                for dz in range(2):
                    row, col = (2 * z + dz + 1) * NB, (2 * y + dy + 1) * L
                    tile = jnp.where(wz == 4.0 * dy + 2.0 * dz, ez, 0.0).astype(bf16)
                    g1[row : row + NB, col : col + L] = tile

    rim1 = rim(g1, NB, FY, FZ, 16)
    start(rim1)

    finish(rim_v)
    for side in range(2):
        for i in range(NC):
            put_volume(vh[side, i].astype(f32), i, side * (FY + 1) * L)
        for y in range(FY + 2):
            here = vz[side, y].astype(f32)
            layers = [moved(here, 1), here, moved(here, -1), jnp.zeros_like(here)]
            row = rows1 + side * NB
            v3[row : row + NB, y * L : (y + 1) * L] = jnp.concatenate(layers, axis=0).astype(bf16)

    count = rows1 + 2 * NB
    c = iota((NB, count), 1)
    z_of = jnp.where(c < rows1, c % FZ, jnp.where(c < rows1 + NB, -1, FZ))
    r, c = iota((count, L), 0), iota((count, L), 1)
    q = jnp.where(r < rows1, r // FZ, (r - rows1) % NB)
    lanes = one_hot(jnp.logical_and(q < 3 * NC, c == (q % NC) * 27 + q // NC))
    line = None
    for ty in range(3):
        part = dot_t(g1[NB : (FZ + 1) * NB, L : (FY + 1) * L], v3[:, ty * L : (ty + FY) * L])
        taps = []
        for tz in range(3):
            tap = None
            for z in range(FZ):
                add = jnp.where(z_of == z + tz - 1, part[z * NB : (z + 1) * NB], 0.0)
                tap = add if tap is None else tap + add
            taps.append(tap)
        taps = exactly(jnp.concatenate(taps, axis=0) * scales[0], lanes)
        for tz in range(3):
            tap = taps[tz * NB : (tz + 1) * NB]
            shift = (ty * 3 + tz) * 3
            tap = pltpu.roll(tap, shift, 1) if shift else tap
            line = tap if line is None else line + tap
    for k in range(ndp):
        for o in range(per1):
            row = k * per1 + o
            msg1[k, :, o * L : (o + 1) * L] = line[row : row + 1]

    scatter1 = scatter(lambda k: msg1.at[k], rz1, ndp)

    finish(rim1)

    total = None
    for ty in range(3):
        part = dot(w1[ty * rows1 : (ty + 1) * rows1, :], g1[:, (2 - ty) * L : (2 - ty + FY) * L])
        total = part if total is None else total + part
    third = NC * FZ
    low = spread_across_x(total[:third], -1)
    high = spread_across_x(total[2 * third :], 1)
    for y in range(FY):
        value = total[third : 2 * third, y * L : (y + 1) * L] + low[y] + high[y]
        for i in range(NC):
            grad_vol[i, y] = value[i * FZ : (i + 1) * FZ].astype(bf16)

    wide2 = pl.cdiv(out2.shape[0], L) * L
    r, c = iota((msg2.shape[1], wide2), 0), iota((msg2.shape[1], wide2), 1)
    of_row = (r // (3 * NB) * NB + r % NB) * 27 + r % (3 * NB) // NB
    to_main = one_hot(jnp.logical_and(r < behind, c == of_row))
    to_last = [
        one_hot(jnp.logical_and((r - behind) // NB == group, c == r % NB * 27))
        for group in range(pl.cdiv(3 * per2, 8))
    ]

    here = gy * ngz + gz

    def share(value, slots, base):
        slots[here] = value
        copies = []
        for index, (y, z) in enumerate(plane):
            copy = remote(slots.at[here], slots.at[here], sem_p, base + index, device(y=y, z=z))
            copy.start()
            copies.append(copy)
        return copies

    def gather(copies, slots):
        for copy in copies:
            copy.wait()
        value = slots[0]
        for d in range(1, ngy * ngz):
            value = value + slots[d]
        return value

    def reduce(copies, own, slots):
        for copy in copies:
            copy.wait()
        for d in range(1, ndp):
            own = own + slots[d]
        return own

    if far:
        pl.semaphore_wait(sem_r.at[2], len(far))
    own = msg2[pl.ds(pl.multiple_of(dp * 8, 8), 8), :]
    share2 = share(reduce(scatter2, own, rz2), rp2, 0)
    share1 = share(reduce(scatter1, msg1[dp], rz1), rp1, len(plane))

    sums = gather(share2, rp2)
    main = exactly(sums, to_main)
    line = None
    for tap in range(8):
        row = main[tap : tap + 1]
        row = pltpu.roll(row, 3 * tap, 1) if tap else row
        line = row if line is None else line + row
    last = [exactly(sums, lanes) for lanes in to_last]
    for piece in range(3 * per2):
        row = last[piece // 8][piece % 8 : piece % 8 + 1]
        line = line + pltpu.roll(row, piece // 3 * NB * 27 + 24 + piece % 3, 1)
    out2[...] = line[0, : out2.shape[0]]
    line = gather(share1, rp1)
    for o in range(per1):
        out1[o * NC * 27 : (o + 1) * NC * 27] = line[0, o * L : o * L + NC * 27]


def reach(ndp):
    return max(1, ndp // 4)


def handed_on(*refs):
    sources, targets, held, sems = refs[:3], refs[3:6], refs[6:9], refs[9]
    loads = [pltpu.make_async_copy(sources[n], held[n], sems.at[0, n]) for n in range(3)]
    stores = [pltpu.make_async_copy(held[n], targets[n], sems.at[1, n]) for n in range(3)]
    for load in loads:
        load.start()
    for load, store in zip(loads, stores):
        load.wait()
        store.start()
    for store in stores:
        store.wait()


def shards(sizes, scales, volume, first, where_first, second, where_second, upstream, k1, k2):
    ndp, ngy, ngz = sizes
    k1 = jnp.transpose(k1, (2, 3, 4, 1, 0)).reshape(27, NC, NB)
    k2 = jnp.transpose(k2, (2, 3, 4, 1, 0)).reshape(27 * NB, NA)
    per2, per1 = NA // ndp, NB // ndp
    wide1 = per1 * L
    wide2 = pl.cdiv(per2 * 3 * NB + pl.cdiv(3 * per2, 8) * NB, L) * L
    there = ngy * ngz
    vmem = pl.BlockSpec(memory_space=pltpu.VMEM)
    arguments = (
        volume[0],
        first[0],
        where_first[0],
        second[0, :, 0],
        where_second[0, :, 0],
        upstream[0, :, 0],
        k1,
        k2,
    )
    results = pl.pallas_call(
        functools.partial(kernel, sizes, scales),
        out_shape=(
            jax.ShapeDtypeStruct((NC, FY, FZ, L), bf16),
            jax.ShapeDtypeStruct((per1 * NC * 27,), f32),
            jax.ShapeDtypeStruct((per2 * NB * 27,), f32),
        ),
        in_specs=[pl.BlockSpec(memory_space=pltpu.HBM)] * 8,
        out_specs=(vmem,) * 3,
        scratch_shapes=[
            pltpu.VMEM(((HZ + 2) * NA, (HY + 2) * L), bf16),
            pltpu.VMEM(((FZ + 2) * NB, (FY + 2) * L), bf16),
            pltpu.VMEM((9 * HZ * NB, (HZ + 2) * NA), bf16),
            pltpu.VMEM((9 * NC * FZ, (FZ + 2) * NB), bf16),
            pltpu.VMEM((HZ * 3 * NB, HY * L), bf16),
            pltpu.VMEM((3 * NC * FZ + 2 * NB, (FY + 2) * L), bf16),
            pltpu.VMEM((2, FY, NC, L), bf16),
            pltpu.VMEM((2, NC, FZ, L), bf16),
            pltpu.VMEM((2, FY + 2, NC, L), bf16),
            pltpu.VMEM((2, HZ // 2 * NA, L), bf16),
            pltpu.VMEM((2, NA, L), bf16),
            pltpu.VMEM((2, HZ // 2 * NA, L), bf16),
            pltpu.VMEM((2, NA, L), bf16),
            pltpu.VMEM((9 * NA, L), f32),
            pltpu.VMEM((ndp, 1, wide1), f32),
            pltpu.VMEM((ndp * 8, wide2), f32),
            pltpu.VMEM((ndp, 1, wide1), f32),
            pltpu.VMEM((ndp, 8, wide2), f32),
            pltpu.VMEM((there, 1, wide1), f32),
            pltpu.VMEM((there, 8, wide2), f32),
            pltpu.SemaphoreType.DMA((2, 24)),
            pltpu.SemaphoreType.DMA((2, 2 * ndp)),
            pltpu.SemaphoreType.DMA((2, 2 * there)),
            pltpu.SemaphoreType.REGULAR((3,)),
            *[pltpu.VMEM(one.shape, one.dtype) for one in arguments],
            pltpu.SemaphoreType.DMA((8,)),
        ],
        compiler_params=pltpu.CompilerParams(collective_id=0, has_side_effects=True),
    )(*arguments)
    grad_vol, first_out, second_out = pl.pallas_call(
        handed_on,
        out_shape=tuple(jax.ShapeDtypeStruct(one.shape, one.dtype) for one in results),
        in_specs=[pl.BlockSpec(memory_space=pltpu.HBM)] * 3,
        out_specs=(pl.BlockSpec(memory_space=pltpu.HBM),) * 3,
        scratch_shapes=[pltpu.VMEM(one.shape, one.dtype) for one in results]
        + [pltpu.SemaphoreType.DMA((2, 3))],

    )(*results)
    return (grad_vol[None], first_out, second_out)


def solution(mesh):
    sizes = tuple(mesh.shape[axis] for axis in ("dp", "gy", "gz"))
    cells = sizes[0] * sizes[1] * sizes[2] * FY * FZ * L
    scales = (math.sqrt(8.0 / cells), math.sqrt(64.0 / cells))
    split = P("dp", None, "gy", "gz", None)
    return jax.shard_map(
        functools.partial(shards, sizes, scales),
        mesh=mesh,
        in_specs=(split,) * 6 + (P(), P()),
        out_specs=(split, P("dp"), P("dp")),
        check_vma=False,
    )
```
